256 devices in a mesh: row: 8 (over z_hi, core), col: 32 (over y, x, z_lo).
Axes of the slice: x: 4, y: 4, z: 8 (z_hi: 4, z_lo: 2; z = z_hi * 2 + z_lo), core: 2. Of those that a mesh axis runs over, the one named last changes fastest.
Arguments:
- pair: bfloat16 [1536, 1536, 128], P('row', 'col'), may hold values from -6 to 6
- seq: bfloat16 [1536, 1024], P(None, 'col'), may hold values from -6 to 6
- w_hidden: bfloat16 [128, 512], replicated, may hold values from -0.5 to 0.5
- w_back: bfloat16 [512, 128], replicated, may hold values from -0.25 to 0.25
- w_bias: bfloat16 [128, 32], replicated, may hold values from -0.5 to 0.5
- w_query: bfloat16 [1024, 1024], replicated, may hold values from -10 to 10
- w_key: bfloat16 [1024, 1024], replicated, may hold values from -0.1875 to 0.1875
- w_value: bfloat16 [1024, 1024], replicated, may hold values from -0.1875 to 0.1875
- w_out: bfloat16 [1024, 1024], replicated, may hold values from -0.1875 to 0.1875
- w_project: bfloat16 [1024, 128], replicated, may hold values from -0.1875 to 0.1875
- w_pair: bfloat16 [128, 128], replicated, may hold values from -0.5 to 0.5
Outputs:
- pair_out: bfloat16 [1536, 1536, 128], P('row', 'col')
- seq_new: bfloat16 [1536, 1024], P('row', 'col')
The draws below stay inside these ranges and needn't reach their ends.
All inputs are finite; a program needn't handle non-finite values.
Results may differ from the reference program's by a relative error of at most 0.013.
The reference program's roundings to bfloat16 on the way count: a program that leaves them out, or rounds other values in their place, can miss the bound.
Values may be sent and summed in bfloat16 or wider, within the bound.
A program may use at most 128 MiB of HBM per device.

```python
import jax
import jax.numpy as jnp
from jax import lax

D = 1024
HEADS = 32
C = 128
PH = 512
L = 1536
N_ROW = 8


def draw_w_query(key, part):
    base = jax.random.truncated_normal(key, -4.0, 4.0, (D, D), jnp.float32) * D ** (-0.5)
    return base.astype(jnp.bfloat16)


def block_scale(stream_key, shape, shards, smallest, top_value):
    def one(dim, shards_of):
        heights = jax.random.uniform(jax.random.fold_in(jax.random.fold_in(stream_key, 6), dim), (shards_of,), jnp.float32, smallest / len(shards), top_value / len(shards))
        return jnp.repeat(jnp.exp(heights), shape[dim] // shards_of).reshape((-1,) + (1,) * (len(shape) - dim - 1))

    level = one(*shards[0])
    for cut in shards[1:]:
        level = level * one(*cut)
    return level


def scatter_about(stream_key, extent, width, reach, cuts=(), held_as=jnp.bfloat16):
    array = jax.random.normal(stream_key, extent, jnp.float32) * width
    if len(cuts) > 0:
        array = block_scale(stream_key, extent, cuts, -0.22, 0.18) * array
    return jnp.clip(array, min=-reach, max=reach).astype(held_as)


def setup_inputs(seed: int = 0) -> dict:
    seeds = jax.random.split(jax.random.key(seed), 12)
    pair = scatter_about(seeds[0], (L, L, C), 1.0, 6.0, ((0, 8), (1, 32)))
    seq = scatter_about(seeds[1], (L, D), 1.0, 6.0, ((1, 32),))
    w_hidden = scatter_about(seeds[2], (C, PH), C ** -0.5, 0.5)
    w_back = scatter_about(seeds[3], (PH, C), PH ** -0.5, 0.25)
    w_bias = scatter_about(seeds[4], (C, HEADS), C ** -0.5, 0.5)
    w_query = draw_w_query(jax.random.fold_in(seeds[11], 71), 0)
    w_key = scatter_about(seeds[6], (D, D), D ** -0.5, 0.1875)
    w_value = scatter_about(seeds[7], (D, D), D ** -0.5, 0.1875)
    w_out = scatter_about(seeds[8], (D, D), D ** -0.5, 0.1875)
    w_project = scatter_about(seeds[9], (D, C), D ** -0.5, 0.1875)
    w_pair = scatter_about(seeds[10], (C, C), C ** -0.5, 0.5)
    return dict(pair=pair, seq=seq, w_hidden=w_hidden, w_back=w_back, w_bias=w_bias, w_query=w_query, w_key=w_key, w_value=w_value, w_out=w_out, w_project=w_project, w_pair=w_pair)


eps_norm = 1e-05

def layer_norm(values_in):
    row_mean = lax.optimization_barrier(jnp.mean(values_in, axis=-1, keepdims=True))
    centred = values_in - row_mean
    row_var = lax.optimization_barrier(jnp.mean(centred * centred, axis=-1, keepdims=True))
    return centred * lax.rsqrt(row_var + eps_norm)

def reference(pair, seq, w_hidden, w_back, w_bias, w_query, w_key, w_value, w_out, w_project, w_pair):
    f32 = jnp.float32
    bf16 = jnp.bfloat16
    highest = lax.Precision.HIGHEST
    row_span = L // N_ROW
    head_dim = D // HEADS
    half = C // 2
    seq_norm = layer_norm(seq.astype(f32)).astype(bf16)
    queries = jnp.dot(seq_norm, w_query, preferred_element_type=f32).astype(bf16)
    keys_proj = jnp.dot(seq_norm, w_key, preferred_element_type=f32).astype(bf16)
    values_proj = jnp.dot(seq_norm, w_value, preferred_element_type=f32).astype(bf16)
    keys_f = keys_proj.astype(f32).reshape(L, HEADS, head_dim)
    values_f = values_proj.astype(f32).reshape(L, HEADS, head_dim)

    def first_pass(inputs):
        pair_rows, query_rows, seq_rows = inputs
        normed = layer_norm(pair_rows.astype(f32)).astype(bf16).reshape(-1, C)
        hidden = jax.nn.relu(jnp.dot(normed, w_hidden, preferred_element_type=f32)).astype(bf16)
        pair_mid = (pair_rows.astype(f32) + jnp.dot(hidden, w_back, preferred_element_type=f32).reshape(row_span, L, C)).astype(bf16)
        mid_norm = layer_norm(pair_mid.astype(f32)).astype(bf16).reshape(-1, C)
        pair_bias = jnp.dot(mid_norm, w_bias, preferred_element_type=f32).reshape(row_span, L, HEADS).transpose(2, 0, 1)
        query_f = query_rows.astype(f32).reshape(row_span, HEADS, head_dim)
        scores = jnp.einsum('ihd,jhd->hij', query_f, keys_f, precision=highest) * head_dim ** (-0.5) + pair_bias
        row_top = lax.optimization_barrier(jnp.max(scores, axis=2, keepdims=True))
        weights = jnp.exp(scores - row_top)
        denom_sum = lax.optimization_barrier(jnp.sum(weights, axis=2))
        weighted = jnp.einsum('hij,jhd->ihd', weights, values_f, precision=highest)
        attended = (weighted / denom_sum.T[:, :, None]).reshape(row_span, D).astype(bf16)
        seq_next = (seq_rows.astype(f32) + jnp.dot(attended, w_out, preferred_element_type=f32)).astype(bf16)
        projected = jnp.dot(layer_norm(seq_next.astype(f32)).astype(bf16), w_project, preferred_element_type=f32).astype(bf16)
        return (pair_mid, seq_next, projected)
    pair_mid, seq_next, projected = lax.map(first_pass, (pair.reshape(N_ROW, row_span, L, C), queries.reshape(N_ROW, row_span, D), seq.reshape(N_ROW, row_span, D)))
    right_proj = projected.reshape(L, C)[:, half:].astype(f32)

    def second_pass(inputs):
        mid_rows, proj_rows = inputs
        left_proj = proj_rows[:, :half].astype(f32)
        product = left_proj[:, None, :] * right_proj[None, :, :]
        difference = left_proj[:, None, :] - right_proj[None, :, :]
        feature = jnp.concatenate([product, difference], axis=-1).astype(bf16).reshape(-1, C)
        return (mid_rows.astype(f32) + jnp.dot(feature, w_pair, preferred_element_type=f32).reshape(row_span, L, C)).astype(bf16)
    pair_out = lax.map(second_pass, (pair_mid, projected)).reshape(L, L, C)
    return (pair_out, seq_next.reshape(L, D))
```

```python
import functools

import jax
import jax.numpy as jnp
from jax import lax
from jax.experimental import pallas as pl
from jax.experimental.pallas import tpu as pltpu
from jax.sharding import PartitionSpec as P

HEADS = 32
EPS = 1e-05
F32 = jnp.float32
BF16 = jnp.bfloat16

R_DEV, C_DEV = 8, 32
NI, NJ, C, D, PH = 192, 48, 128, 1024, 512
OWNERS, OWN = 24, 8
WL = D + 128
RC = 16
SCALE = 32 ** (-0.5)
MESH = pl.DeviceIdType.MESH


def nt(a, b):
    return lax.dot_general(a, b, (((1,), (1,)), ((), ())), preferred_element_type=F32)


def nn(a, b):
    return jnp.dot(a, b, preferred_element_type=F32)


def layer_norm(x, axis=-1):
    mean = jnp.mean(x, axis=axis, keepdims=True)
    cen = x - mean
    var = jnp.mean(cen * cen, axis=axis, keepdims=True)
    return cen * lax.rsqrt(var + EPS)


def iota(shape, dim):
    return lax.broadcasted_iota(jnp.int32, shape, dim)


def owner_of(col):
    y, x, z = col // 8, (col // 2) % 4, col % 2
    xr = jnp.where(x > y, x - 1, x)
    return (y * 3 + xr) * 2 + z, x != y, y


def col_of(y, t):
    xr, z = t // 2, t % 2
    x = jnp.where(xr >= y, xr + 1, xr)
    return (y * 4 + x) * 2 + z


def main_kernel(
    pair_h, seq_h, whid_h, wback_h, wbias_h, wq_h, wk_h, wv_h, wout_h, wproj_h,
    mid_h, left_o, right_o, seq_o,
    pair_v, mid_v, mn_v, bias_v, bmat_v, seq_v, whid_v, wback_v, wbias_v, wq_v, wk_v, wv_v, wout_v, wproj_v,
    msgs, sqk, q_v, kv_v, kbd, vbd, w_v, wmsg, wrecv, emsg, erecv, rmsg, rrecv,
    in_sem, pin_sem, mid_sem, s_send, s_recv, w_send, w_recv, e_send, e_recv, r_send, r_recv,
):
    me_r, me_c = lax.axis_index("row"), lax.axis_index("col")
    own_o, is_owner, me_y = owner_of(me_c)
    own_o = jnp.where(is_owner, own_o, 0)
    dest_c = 4 * me_r + me_y
    self_right = jnp.logical_and(is_owner, dest_c == me_c)

    barrier = pltpu.get_barrier_semaphore()

    def greet(s, _):
        pl.semaphore_signal(barrier, 1, device_id=(me_r, (me_c + s) % C_DEV), device_id_type=MESH)
        return 0

    lax.fori_loop(1, C_DEV, greet, 0)
    src_r, src_y = me_c // 4, me_c % 4

    def greet_right(t, _):
        src = col_of(src_y, t)

        @pl.when(jnp.logical_not(jnp.logical_and(src_r == me_r, src == me_c)))
        def _():
            pl.semaphore_signal(barrier, 1, device_id=(src_r, src), device_id_type=MESH)

        return 0

    lax.fori_loop(0, 6, greet_right, 0)

    def load(src, dst, k):
        cp = pltpu.make_async_copy(src, dst, in_sem.at[k])
        cp.start()
        return cp

    c_seq = load(seq_h, seq_v, 0)
    c_hid = load(whid_h, whid_v, 1)
    c_back = load(wback_h, wback_v, 2)
    c_bias = load(wbias_h, wbias_v, 3)
    n_steps = NI // RC
    pair_in = []
    for k in range(n_steps):
        rows = pl.ds(k * RC, RC)
        cp = pltpu.make_async_copy(pair_h.at[rows], pair_v.at[rows], pin_sem.at[k])
        cp.start()
        pair_in.append(cp)
    c_q = load(wq_h, wq_v, 4)
    c_k = load(wk_h, wk_v, 5)
    c_v = load(wv_h, wv_v, 6)
    c_out = load(wout_h, wout_v, 7)
    c_proj = load(wproj_h, wproj_v, 8)

    c_seq.wait()
    eye = jnp.where(iota((32, 32), 0) == iota((32, 32), 1), 1.0, 0.0).astype(BF16)
    own_rows = seq_v[pl.ds(pl.multiple_of(me_r * NI, 64), NI), :]
    first = nt(eye, own_rows[:128]).astype(BF16)
    tail = own_rows[128:]
    pad = jnp.zeros((16, 32), BF16)

    def message(s, _):
        dst = (me_c + s) % C_DEV
        keys = seq_v[pl.ds(pl.multiple_of(dst * NJ, 16), NJ), :]
        second = nt(eye, jnp.concatenate([tail, keys, pad], axis=0)).astype(BF16)
        msgs[dst, :, 0:128] = first
        msgs[dst, :, 128:256] = second
        return 0

    lax.fori_loop(0, C_DEV, message, 0)

    pl.semaphore_wait(
        barrier, C_DEV - 1 + jnp.where(is_owner, R_DEV, 0) - jnp.where(self_right, 1, 0)
    )
    my_slab = pl.ds(pl.multiple_of(me_c * 32, 32), 32)

    def send_seq(s, _):
        dst = (me_c + s) % C_DEV
        pltpu.make_async_remote_copy(
            msgs.at[dst], sqk.at[my_slab], s_send, s_recv, device_id=(me_r, dst), device_id_type=MESH
        ).start()
        return 0

    lax.fori_loop(1, C_DEV, send_seq, 0)
    pltpu.make_async_copy(msgs.at[me_c], sqk.at[my_slab], s_recv).start()

    c_bias.wait()
    spread = jnp.where(
        iota((32, 256), 0) == (iota((32, 256), 1) // 128) * 16 + iota((32, 256), 1) % 16, 1.0, 0.0
    ).astype(BF16)
    wide = nn(wbias_v[...], spread)
    slot = (iota((C, 256), 1) % 128) // 16
    for j8 in range(8):
        bmat_v[j8 * C : (j8 + 1) * C, :] = jnp.where(slot == j8, wide, 0.0).astype(BF16)

    c_hid.wait()
    c_back.wait()

    def pair_step(k, _):
        i0 = pl.multiple_of(k * RC, RC)
        rows = pl.ds(i0, RC)
        pltpu.make_async_copy(pair_h.at[rows], pair_v.at[rows], pin_sem.at[k]).wait()
        x = pair_v[rows].astype(F32).reshape(RC * NJ, C)
        hid = jnp.maximum(nn(layer_norm(x).astype(BF16), whid_v[...]), 0.0).astype(BF16)
        mid = (x + nn(hid, wback_v[...])).astype(BF16)
        mid_v[rows] = mid.reshape(RC, NJ, C)
        mn_v[...] = layer_norm(mid.astype(F32))
        blocks = []
        for jb in range(6):
            cols = []
            for j8 in range(8):
                j = jb * 8 + j8
                cols.append(
                    jnp.concatenate(
                        [mn_v[pl.ds(h * 8 * NJ + j, 8, stride=NJ), :] for h in range(RC // 8)], axis=0
                    ).astype(BF16)
                )
            blocks.append(jnp.concatenate(cols, axis=1))
        out = nn(jnp.concatenate(blocks, axis=0), bmat_v[...])
        for jb in range(6):
            for g in range(2):
                bias_v[g, jb, rows, :] = out[jb * RC : (jb + 1) * RC, g * 128 : (g + 1) * 128]
        pltpu.make_async_copy(mid_v.at[rows], mid_h.at[rows], mid_sem).start()
        return 0

    lax.fori_loop(0, n_steps, pair_step, 0)

    pltpu.make_async_copy(sqk, sqk, s_recv).wait()
    ident = jnp.where(iota((256, 256), 0) == iota((256, 256), 1), 1.0, 0.0).astype(BF16)
    normed = nt(ident, layer_norm(sqk[...].astype(F32), 0).astype(BF16)).astype(BF16)
    c_q.wait()
    q_v[...] = nn(normed[:NI], wq_v[...]).astype(BF16)
    c_k.wait()
    c_v.wait()
    kv_v[:, 0:D] = nn(normed[NI : NI + NJ], wk_v[...])
    kv_v[:, D : 2 * D] = nn(normed[NI : NI + NJ], wv_v[...])
    head_here = iota((16, 512), 0) == iota((16, 512), 1) // 32

    def spread_keys(j, _):
        dst = pl.ds(pl.multiple_of(j * 16, 16), 16)
        for g in range(2):
            krow = jnp.broadcast_to(kv_v[pl.ds(j, 1), g * 512 : (g + 1) * 512], (16, 512))
            vrow = jnp.broadcast_to(kv_v[pl.ds(j, 1), D + g * 512 : D + (g + 1) * 512], (16, 512))
            kbd[g, dst, :] = jnp.where(head_here, krow, 0.0).astype(BF16)
            vbd[g, dst, :] = jnp.where(head_here, vrow, 0.0).astype(BF16)
        return 0

    lax.fori_loop(0, NJ, spread_keys, 0)

    lane = iota((NI, 128), 1)
    parts = []
    for g in range(2):
        scores = nt(q_v[:, g * 512 : (g + 1) * 512], kbd[g])
        tiles = [scores[:, jb * 128 : (jb + 1) * 128] * SCALE + bias_v[g, jb] for jb in range(6)]
        top = functools.reduce(jnp.maximum, tiles)
        for shift in (16, 32, 64):
            top = jnp.maximum(top, pltpu.roll(top, shift, 1))
        total = None
        for jb in range(6):
            w = jnp.exp(tiles[jb] - top)
            w_v[g, :, jb * 128 : (jb + 1) * 128] = w.astype(BF16)
            total = w if total is None else total + w
        for shift in (16, 32, 64):
            total = total + pltpu.roll(total, shift, 1)
        weighted = nn(w_v[g], vbd[g])
        wmsg[:, :, g * 512 : (g + 1) * 512] = weighted.reshape(OWNERS, OWN, 512).astype(BF16)
        high = top.astype(BF16).astype(F32)
        middle = (top - high).astype(BF16).astype(F32)
        low = (top - high) - middle
        parts.append((high, middle, low, total))
    stats = jnp.zeros((NI, 128), F32)
    for p in range(4):
        for g in range(2):
            stats = jnp.where(lane // 16 == p * 2 + g, parts[g][p], stats)
    wmsg[:, :, D:WL] = stats.reshape(OWNERS, OWN, 128).astype(BF16)

    def send_rows(s, _):
        dst = (me_c + s) % C_DEV
        o, owns, _y = owner_of(dst)

        @pl.when(owns)
        def _():
            pltpu.make_async_remote_copy(
                wmsg.at[o], wrecv.at[me_c], w_send, w_recv, device_id=(me_r, dst), device_id_type=MESH
            ).start()

        return 0

    lax.fori_loop(1, C_DEV, send_rows, 0)

    @pl.when(is_owner)
    def _():
        pltpu.make_async_copy(wmsg.at[own_o], wrecv.at[me_c], w_recv).start()
        pick = jnp.where(iota((8, 256), 1) == own_o * 8 + iota((8, 256), 0), 1.0, 0.0).astype(BF16)
        resid = nt(pick, sqk[...])
        head_lane = iota((128, D), 0) == iota((128, D), 1) // 32
        expand = jnp.where(head_lane, 1.0, 0.0).astype(BF16)
        c_out.wait()
        c_proj.wait()
        pltpu.make_async_copy(wrecv, wrecv, w_recv).wait()
        st = wrecv[:, :, D:WL].astype(F32).reshape(C_DEV * OWN, 128)
        m = (st + pltpu.roll(st, 96, 1)) + pltpu.roll(st, 64, 1)
        den = pltpu.roll(st, 32, 1)
        m3 = m.reshape(C_DEV, OWN, 128)
        top = jnp.max(m3, axis=0)
        fac = jnp.where(iota((C_DEV, OWN, 128), 2) < 32, jnp.exp(jnp.minimum(m3 - top[None], 0.0)), 0.0)
        whole = jnp.sum(fac * den.reshape(C_DEV, OWN, 128), axis=0)
        whole = jnp.where(iota((OWN, 128), 1) < 32, whole, 1.0)
        fac = (fac / whole[None]).reshape(C_DEV * OWN, 128)
        high = fac.astype(BF16)
        low = (fac - high.astype(F32)).astype(BF16)
        wide = (nn(high, expand) + nn(low, expand)).reshape(C_DEV, OWN, D)
        attended = jnp.sum(wide * wrecv[:, :, 0:D].astype(F32), axis=0).astype(BF16)
        seq_new = (resid + nn(attended, wout_v[...])).astype(BF16).astype(F32)
        proj = nn(layer_norm(seq_new).astype(BF16), wproj_v[...]).astype(BF16).astype(F32)
        turned = pltpu.roll(proj, 64, 1)
        lane8 = iota((OWN, 128), 1)
        left = jnp.where(lane8 < 64, proj, turned).astype(BF16)
        right = jnp.where(lane8 < 64, turned, proj).astype(BF16)
        rmsg[...] = right
        for c in range(C_DEV):
            tile = seq_new[:, (c // 4) * 128 : (c // 4) * 128 + 128]
            if c % 4:
                tile = pltpu.roll(tile, 128 - 32 * (c % 4), 1)
            emsg[c, 0] = left
            emsg[c, 1] = tile.astype(BF16)

        def send_right(r, _):
            here = jnp.logical_and(r == me_r, dest_c == me_c)

            @pl.when(jnp.logical_not(here))
            def _():
                pltpu.make_async_remote_copy(
                    rmsg, rrecv.at[own_o % 6], r_send, r_recv, device_id=(r, dest_c), device_id_type=MESH
                ).start()

            @pl.when(here)
            def _():
                pltpu.make_async_copy(rmsg, rrecv.at[own_o % 6], r_recv).start()

            return 0

        lax.fori_loop(0, R_DEV, send_right, 0)

        def send_left(s, _):
            dst = (me_c + s) % C_DEV
            pltpu.make_async_remote_copy(
                emsg.at[dst], erecv.at[own_o], e_send, e_recv, device_id=(me_r, dst), device_id_type=MESH
            ).start()
            return 0

        lax.fori_loop(1, C_DEV, send_left, 0)
        pltpu.make_async_copy(emsg.at[me_c], erecv.at[own_o], e_recv).start()

    @pl.when(jnp.logical_not(is_owner))
    def _():
        c_out.wait()
        c_proj.wait()

    pltpu.make_async_copy(mid_v, mid_h, mid_sem).wait()
    pltpu.make_async_copy(rrecv, rrecv, r_recv).wait()
    right_o[...] = rrecv[...].astype(F32).reshape(NJ, 128)
    pltpu.make_async_copy(erecv, erecv, e_recv).wait()
    left_o[...] = erecv[:, 0].astype(F32).reshape(NI, 128)
    seq_o[...] = erecv[:, 1].astype(F32).reshape(NI, 128)[:, 0:32].astype(BF16)

    pltpu.make_async_copy(msgs.at[0 : C_DEV - 1], msgs.at[0 : C_DEV - 1], s_send).wait()

    def sent_rows(s, _):
        o, owns, _y = owner_of((me_c + s) % C_DEV)

        @pl.when(owns)
        def _():
            pltpu.make_async_copy(wmsg.at[o], wmsg.at[o], w_send).wait()

        return 0

    lax.fori_loop(1, C_DEV, sent_rows, 0)

    @pl.when(is_owner)
    def _():
        pltpu.make_async_copy(emsg.at[0 : C_DEV - 1], emsg.at[0 : C_DEV - 1], e_send).wait()

        def sent_right(r, _):
            @pl.when(jnp.logical_not(jnp.logical_and(r == me_r, dest_c == me_c)))
            def _():
                pltpu.make_async_copy(rmsg, rmsg, r_send).wait()

            return 0

        lax.fori_loop(0, R_DEV, sent_right, 0)


def pair_kernel(mid_ref, left_ref, right_ref, wpair_ref, out_ref):
    n = mid_ref.shape[0]
    lane = iota((NJ, C), 1)
    right = right_ref[...]
    scale = jnp.where(lane < 64, right, 1.0)
    shift = jnp.where(lane < 64, 0.0, -right)
    left = left_ref[...].reshape(n, 1, C)
    feature = (left * scale[None] + shift[None]).astype(BF16).reshape(n * NJ, C)
    update = nn(feature, wpair_ref[...])
    mid = mid_ref[...].astype(F32).reshape(n * NJ, C)
    out_ref[...] = (mid + update).astype(BF16).reshape(n, NJ, C)


def local(pair, seq, w_hidden, w_back, w_bias, w_query, w_key, w_value, w_out, w_project, w_pair):
    hbm = pl.BlockSpec(memory_space=pl.ANY)
    vmem = pl.BlockSpec(memory_space=pltpu.VMEM)
    dma = pltpu.SemaphoreType.DMA
    mid, left, right, seq_new = pl.pallas_call(
        main_kernel,
        out_shape=(
            jax.ShapeDtypeStruct((NI, NJ, C), BF16),
            jax.ShapeDtypeStruct((NI, 128), F32),
            jax.ShapeDtypeStruct((NJ, 128), F32),
            jax.ShapeDtypeStruct((NI, 32), BF16),
        ),
        in_specs=[hbm] * 10,
        out_specs=(hbm, vmem, vmem, vmem),
        scratch_shapes=[
            pltpu.VMEM((NI, NJ, C), BF16),
            pltpu.VMEM((NI, NJ, C), BF16),
            pltpu.VMEM((RC * NJ, C), F32),
            pltpu.VMEM((2, 6, NI, 128), F32),
            pltpu.VMEM((8 * C, 256), BF16),
            pltpu.VMEM((R_DEV * NI, 32), BF16),
            pltpu.VMEM((C, PH), BF16),
            pltpu.VMEM((PH, C), BF16),
            pltpu.VMEM((C, HEADS), BF16),
            pltpu.VMEM((D, D), BF16),
            pltpu.VMEM((D, D), BF16),
            pltpu.VMEM((D, D), BF16),
            pltpu.VMEM((D, D), BF16),
            pltpu.VMEM((D, C), BF16),
            pltpu.VMEM((C_DEV, 32, 256), BF16),
            pltpu.VMEM((D, 256), BF16),
            pltpu.VMEM((NI, D), BF16),
            pltpu.VMEM((NJ, 2 * D), F32),
            pltpu.VMEM((2, 16 * NJ, 512), BF16),
            pltpu.VMEM((2, 16 * NJ, 512), BF16),
            pltpu.VMEM((2, NI, 16 * NJ), BF16),
            pltpu.VMEM((OWNERS, OWN, WL), BF16),
            pltpu.VMEM((C_DEV, OWN, WL), BF16),
            pltpu.VMEM((C_DEV, 2, OWN, 128), BF16),
            pltpu.VMEM((OWNERS, 2, OWN, 128), BF16),
            pltpu.VMEM((OWN, 128), BF16),
            pltpu.VMEM((6, OWN, 128), BF16),
            dma((9,)),
            dma((NI // RC,)),
            dma, dma, dma, dma, dma, dma, dma, dma, dma,
        ],
        compiler_params=pltpu.CompilerParams(
            collective_id=0, has_side_effects=True, vmem_limit_bytes=60 * 1024 * 1024
        ),
        name="trunk_main",
    )(pair, seq, w_hidden, w_back, w_bias, w_query, w_key, w_value, w_out, w_project)
    step = 16
    pair_out = pl.pallas_call(
        pair_kernel,
        out_shape=jax.ShapeDtypeStruct((NI, NJ, C), BF16),
        grid=(NI // step,),
        in_specs=[
            pl.BlockSpec((step, NJ, C), lambda i: (i, 0, 0)),
            pl.BlockSpec((step, 128), lambda i: (i, 0)),
            pl.BlockSpec((NJ, 128), lambda i: (0, 0)),
            pl.BlockSpec((C, C), lambda i: (0, 0)),
        ],
        out_specs=pl.BlockSpec((step, NJ, C), lambda i: (i, 0, 0)),
        compiler_params=pltpu.CompilerParams(dimension_semantics=("arbitrary",)),
        name="pair_update",
    )(mid, left, right, w_pair)
    return pair_out, seq_new


def solution(mesh):
    return jax.shard_map(
        local,
        mesh=mesh,
        in_specs=(P("row", "col", None), P(None, "col")) + (P(),) * 9,
        out_specs=(P("row", "col", None), P("row", "col")),
        check_vma=False,
    )
```

```python
import functools

import jax
import jax.numpy as jnp
from jax import lax
from jax.experimental import pallas as pl
from jax.experimental.pallas import tpu as pltpu
from jax.sharding import PartitionSpec as P

HEADS = 32
EPS = 1e-05
F32 = jnp.float32
BF16 = jnp.bfloat16

R_DEV, C_DEV = 8, 32
NI, NJ, C, D, PH = 192, 48, 128, 1024, 512
OWNERS, OWN = 24, 8
WL = D + 128
RC = 16
STEPS = NI // RC
BLK = 48
SPB = BLK // RC
KSTEPS = 12
SCALE = 32 ** (-0.5)
MESH = pl.DeviceIdType.MESH


def nt(a, b):
    return lax.dot_general(a, b, (((1,), (1,)), ((), ())), preferred_element_type=F32)


def tn(a, b):
    return lax.dot_general(a, b, (((0,), (0,)), ((), ())), preferred_element_type=F32)


def nn(a, b):
    return jnp.dot(a, b, preferred_element_type=F32)


def layer_norm(x, axis=-1):
    mean = jnp.mean(x, axis=axis, keepdims=True)
    cen = x - mean
    var = jnp.mean(cen * cen, axis=axis, keepdims=True)
    return cen * lax.rsqrt(var + EPS)


def iota(shape, dim):
    return lax.broadcasted_iota(jnp.int32, shape, dim)


def owner_of(col):
    y, x, z = col // 8, (col // 2) % 4, col % 2
    xr = jnp.where(x > y, x - 1, x)
    return (y * 3 + xr) * 2 + z, x != y, y


def col_of(y, t):
    xr, z = t // 2, t % 2
    x = jnp.where(xr >= y, xr + 1, xr)
    return (y * 4 + x) * 2 + z


def main_kernel(
    pair_h, seq_h, whid_h, wback_h, wbias_h, wq_h, wk_h, wv_h, wout_h, wproj_h,
    mid_h, left_o, right_o, seq_o,
    pair_v, mid_v, nb0, nb1, mb0, mb1, mn0, mn1, bias_v, bmat_v,
    seq_v, whid_v, wback_v, wbias_v, wq_v, wk_v, wv_v, wout_v, wproj_v,
    msgs, sqk, sqn, q_v, kv_v, kbd, vbd, w_v, expand_v, wmsg, wrecv, emsg, erecv, rmsg, rrecv,
    in_sem, pin_sem, mid_sem, s_send, s_recv, w_send, w_recv, e_send, e_recv, r_send, r_recv,
):
    me_r, me_c = lax.axis_index("row"), lax.axis_index("col")
    own_o, is_owner, me_y = owner_of(me_c)
    own_o = jnp.where(is_owner, own_o, 0)
    dest_c = 4 * me_r + me_y
    self_right = jnp.logical_and(is_owner, dest_c == me_c)

    barrier = pltpu.get_barrier_semaphore()

    def greet(s, _):
        pl.semaphore_signal(barrier, 1, device_id=(me_r, (me_c + s) % C_DEV), device_id_type=MESH)
        return 0

    lax.fori_loop(1, C_DEV, greet, 0)
    src_r, src_y = me_c // 4, me_c % 4

    def greet_right(t, _):
        src = col_of(src_y, t)

        @pl.when(jnp.logical_not(jnp.logical_and(src_r == me_r, src == me_c)))
        def _():
            pl.semaphore_signal(barrier, 1, device_id=(src_r, src), device_id_type=MESH)

        return 0

    lax.fori_loop(0, 6, greet_right, 0)

    def load(src, dst, k):
        cp = pltpu.make_async_copy(src, dst, in_sem.at[k])
        cp.start()
        return cp

    def block_y(cc):
        return (me_y + 1 + cc) % 4

    def true_rows(k):
        return pl.ds(pl.multiple_of(block_y(k // SPB) * BLK + (k % SPB) * RC, RC), RC)

    c_seq = load(seq_h, seq_v, 0)
    c_hid = load(whid_h, whid_v, 1)
    c_back = load(wback_h, wback_v, 2)
    c_bias = load(wbias_h, wbias_v, 3)

    def pair_copy(k):
        rows = pl.ds(pl.multiple_of(k * RC, RC), RC)
        return pltpu.make_async_copy(pair_h.at[true_rows(k)], pair_v.at[rows], pin_sem.at[k])

    for k in range(STEPS):
        pair_copy(k).start()
    c_q = load(wq_h, wq_v, 4)
    c_k = load(wk_h, wk_v, 5)
    c_v = load(wv_h, wv_v, 6)
    c_out = load(wout_h, wout_v, 7)
    c_proj = load(wproj_h, wproj_v, 8)

    c_seq.wait()
    lane32 = iota((32, 128), 1)
    base = pl.multiple_of((me_r * 3 // 2) * 128, 128)
    own = seq_v[:, pl.ds(base, 256)].astype(F32)
    own = jnp.where(me_r % 2 == 1, pltpu.roll(own, 192, 1), own)
    own0, own1 = own[:, 0:128].astype(BF16), own[:, 128:256]
    for c in range(C_DEV):
        t, o = (c * NJ) // 128, (c * NJ) % 128
        keys = seq_v[:, t * 128 : t * 128 + 128].astype(F32)
        if o + NJ > 128:
            keys = jnp.where(lane32 >= o, keys, seq_v[:, t * 128 + 128 : t * 128 + 256].astype(F32))
        if o != 64:
            keys = pltpu.roll(keys, (64 - o) % 128, 1)
        msgs[c, :, 0:128] = own0
        msgs[c, :, 128:256] = jnp.where(lane32 < 64, own1, jnp.where(lane32 < 112, keys, 0.0)).astype(BF16)

    c_bias.wait()
    spread = jnp.where(
        iota((32, 256), 0) == (iota((32, 256), 1) // 128) * 16 + iota((32, 256), 1) % 16, 1.0, 0.0
    ).astype(BF16)
    wide = tn(wbias_v[...], spread)
    slot = (iota((C, 256), 1) % 128) // 16
    for j8 in range(8):
        bmat_v[j8 * C : (j8 + 1) * C, :] = jnp.where(slot == j8, wide, 0.0).astype(BF16)
    head_lane = iota((128, D), 0) == iota((128, D), 1) // 32
    expand_v[0:128] = jnp.where(head_lane, 1.0, 0.0).astype(BF16)
    expand_v[128:256] = jnp.where(head_lane, 1.0, 0.0).astype(BF16)

    nb, mb, mn = (nb0, nb1), (mb0, mb1), (mn0, mn1)

    def rows_of(k):
        return pl.ds(pl.multiple_of(k * RC, RC), RC)

    def stage_norm(k, s):
        pair_copy(k).wait()
        x = pair_v[rows_of(k)].astype(F32).reshape(RC * NJ, C)
        nb[s][...] = layer_norm(x).astype(BF16)

    def stage_hidden(k, s):
        hid = jnp.maximum(nn(nb[s][...], whid_v[...]), 0.0).astype(BF16)
        x = pair_v[rows_of(k)].astype(F32).reshape(RC * NJ, C)
        mid = (x + nn(hid, wback_v[...])).astype(BF16)
        mid_v[rows_of(k)] = mid.reshape(RC, NJ, C)
        mb[s][...] = mid

    def stage_mid(k, s):
        mn[s][...] = layer_norm(mb[s][...].astype(F32))

    def stage_bias(k, s):
        blocks = []
        for jb in range(6):
            cols = []
            for j8 in range(8):
                j = jb * 8 + j8
                cols.append(
                    jnp.concatenate(
                        [mn[s][pl.ds(h * 8 * NJ + j, 8, stride=NJ), :] for h in range(RC // 8)], axis=0
                    ).astype(BF16)
                )
            blocks.append(jnp.concatenate(cols, axis=1))
        out = nn(jnp.concatenate(blocks, axis=0), bmat_v[...])
        for jb in range(6):
            for g in range(2):
                bias_v[g, jb, rows_of(k), :] = out[jb * RC : (jb + 1) * RC, g * 128 : (g + 1) * 128]

    def mid_out(k):
        return pltpu.make_async_copy(mid_v.at[rows_of(k)], mid_h.at[true_rows(k)], mid_sem)

    def pair_steps(t, _):
        for u in range(2):
            k, s = 2 * t + 1 + u, (1 + u) % 2
            stage_hidden(k, s)
            stage_norm(k + 1, 1 - s)
            stage_mid(k - 1, 1 - s)
            stage_bias(jnp.maximum(k - 2, 0), s)
            mid_out(k - 1).start()
        return 0

    c_hid.wait()
    c_back.wait()
    stage_norm(0, 0)
    stage_hidden(0, 0)
    stage_norm(1, 1)
    mn[1][...] = jnp.zeros_like(mn[1])

    pl.semaphore_wait(
        barrier, C_DEV - 1 + jnp.where(is_owner, R_DEV, 0) - jnp.where(self_right, 1, 0)
    )
    my_slab = pl.ds(pl.multiple_of(me_c * 32, 32), 32)

    def send_seq(s, _):
        dst = (me_c + s) % C_DEV
        pltpu.make_async_remote_copy(
            msgs.at[dst], sqk.at[my_slab], s_send, s_recv, device_id=(me_r, dst), device_id_type=MESH
        ).start()
        return 0

    lax.fori_loop(1, C_DEV, send_seq, 0)
    pltpu.make_async_copy(msgs.at[me_c], sqk.at[my_slab], s_recv).start()

    lax.fori_loop(0, 4, pair_steps, 0)

    pltpu.make_async_copy(sqk, sqk, s_recv).wait()
    CH = 128

    def chunk(k):
        return sqk[pl.ds(pl.multiple_of(k * CH, CH), CH), :].astype(F32).reshape(CH // 8, 8, 256)

    def add_sum(k, acc):
        return acc + jnp.sum(chunk(k), axis=0)

    mean = jnp.sum(lax.fori_loop(0, D // CH, add_sum, jnp.zeros((8, 256), F32)), axis=0, keepdims=True) * (1.0 / D)

    def add_square(k, acc):
        cen = chunk(k) - mean[None]
        return acc + jnp.sum(cen * cen, axis=0)

    var = jnp.sum(lax.fori_loop(0, D // CH, add_square, jnp.zeros((8, 256), F32)), axis=0, keepdims=True) * (1.0 / D)
    inv = lax.rsqrt(var + EPS)

    def norm_chunk(k, _):
        sqn[pl.ds(pl.multiple_of(k * CH, CH), CH), :] = (
            ((chunk(k) - mean[None]) * inv[None]).reshape(CH, 256).astype(BF16)
        )
        return 0

    lax.fori_loop(0, D // CH, norm_chunk, 0)
    ident = jnp.where(iota((256, 256), 0) == iota((256, 256), 1), 1.0, 0.0).astype(BF16)
    normed = nt(ident, sqn[...]).astype(BF16)
    c_q.wait()
    q_v[...] = nn(normed[:NI], wq_v[...]).astype(BF16)
    c_k.wait()
    c_v.wait()
    kv_v[:, 0:D] = nn(normed[NI : NI + NJ], wk_v[...])
    kv_v[:, D : 2 * D] = nn(normed[NI : NI + NJ], wv_v[...])
    head_here = iota((16, 512), 0) == iota((16, 512), 1) // 32

    def spread_keys(j, _):
        dst = pl.ds(pl.multiple_of(j * 16, 16), 16)
        for g in range(2):
            krow = jnp.broadcast_to(kv_v[pl.ds(j, 1), g * 512 : (g + 1) * 512], (16, 512))
            vrow = jnp.broadcast_to(kv_v[pl.ds(j, 1), D + g * 512 : D + (g + 1) * 512], (16, 512))
            kbd[g, dst, :] = jnp.where(head_here, krow, 0.0).astype(BF16)
            vbd[g, dst, :] = jnp.where(head_here, vrow, 0.0).astype(BF16)
        return 0

    lax.fori_loop(0, NJ, spread_keys, 0)

    def attend(first, count):
        n = count * BLK
        lane = iota((n, 128), 1)
        q = [
            q_v[pl.ds(pl.multiple_of(block_y(cc) * BLK, 16), BLK), :] for cc in range(first, first + count)
        ]
        q = q[0] if count == 1 else jnp.concatenate(q, axis=0)
        here = slice(first * BLK, first * BLK + n)
        parts = []
        for g in range(2):
            scores = nt(q[:, g * 512 : (g + 1) * 512], kbd[g])
            tiles = [scores[:, jb * 128 : (jb + 1) * 128] * SCALE + bias_v[g, jb, here, :] for jb in range(6)]
            top = functools.reduce(jnp.maximum, tiles)
            for shift in (16, 32, 64):
                top = jnp.maximum(top, pltpu.roll(top, shift, 1))
            total = None
            for jb in range(6):
                w = jnp.exp(tiles[jb] - top)
                w_v[g, here, jb * 128 : (jb + 1) * 128] = w.astype(BF16)
                total = w if total is None else total + w
            for shift in (16, 32, 64):
                total = total + pltpu.roll(total, shift, 1)
            weighted = nn(w_v[g, here, :], vbd[g])
            wmsg[first * 6 : (first + count) * 6, :, g * 512 : (g + 1) * 512] = weighted.reshape(
                count * 6, OWN, 512
            ).astype(BF16)
            high = top.astype(BF16).astype(F32)
            middle = (top - high).astype(BF16).astype(F32)
            low = (top - high) - middle
            parts.append((high, middle, low, total))
        stats = jnp.zeros((n, 128), F32)
        for p in range(4):
            for g in range(2):
                stats = jnp.where(lane // 16 == p * 2 + g, parts[g][p], stats)
        wmsg[first * 6 : (first + count) * 6, :, D:WL] = stats.reshape(count * 6, OWN, 128).astype(BF16)

        def send_rows(i, _):
            cc, t = first + i // 6, i % 6
            dst = col_of(block_y(cc), t)
            mine = dst == me_c

            @pl.when(jnp.logical_not(mine))
            def _():
                pltpu.make_async_remote_copy(
                    wmsg.at[cc * 6 + t], wrecv.at[me_c], w_send, w_recv,
                    device_id=(me_r, dst), device_id_type=MESH,
                ).start()

            @pl.when(mine)
            def _():
                pltpu.make_async_copy(wmsg.at[cc * 6 + t], wrecv.at[me_c], w_recv).start()

            return 0

        lax.fori_loop(0, count * 6, send_rows, 0)

    attend(0, 2)
    pair_steps(4, 0)
    attend(2, 1)
    stage_hidden(11, 1)
    stage_mid(10, 0)
    stage_bias(9, 1)
    stage_mid(11, 1)
    stage_bias(10, 0)
    stage_bias(11, 1)
    mid_out(10).start()
    mid_out(11).start()
    attend(3, 1)

    @pl.when(is_owner)
    def _():
        pick = jnp.where(iota((8, 256), 1) == own_o * 8 + iota((8, 256), 0), 1.0, 0.0).astype(BF16)
        resid = nt(pick, sqk[...])
        c_out.wait()
        c_proj.wait()
        pltpu.make_async_copy(wrecv, wrecv, w_recv).wait()
        st = wrecv[:, :, D:WL].astype(F32).reshape(C_DEV * OWN, 128)
        m = (st + pltpu.roll(st, 96, 1)) + pltpu.roll(st, 64, 1)
        den = pltpu.roll(st, 32, 1)
        m3 = m.reshape(C_DEV, OWN, 128)
        top = jnp.max(m3, axis=0)
        fac = jnp.where(iota((C_DEV, OWN, 128), 2) < 32, jnp.exp(jnp.minimum(m3 - top[None], 0.0)), 0.0)
        whole = jnp.sum(fac * den.reshape(C_DEV, OWN, 128), axis=0)
        whole = jnp.where(iota((OWN, 128), 1) < 32, whole, 1.0)
        fac = (fac / whole[None]).reshape(C_DEV * OWN, 128)
        high = fac.astype(BF16)
        low = (fac - high.astype(F32)).astype(BF16)
        wide = nn(jnp.concatenate([high, low], axis=1), expand_v[...]).reshape(C_DEV, OWN, D)
        attended = jnp.sum(wide * wrecv[:, :, 0:D].astype(F32), axis=0).astype(BF16)
        seq_new = (resid + nn(attended, wout_v[...])).astype(BF16).astype(F32)
        proj = nn(layer_norm(seq_new).astype(BF16), wproj_v[...]).astype(BF16).astype(F32)
        turned = pltpu.roll(proj, 64, 1)
        lane8 = iota((OWN, 128), 1)
        left = jnp.where(lane8 < 64, proj, turned).astype(BF16)
        right = jnp.where(lane8 < 64, turned, proj).astype(BF16)
        rmsg[...] = right
        for c in range(C_DEV):
            tile = seq_new[:, (c // 4) * 128 : (c // 4) * 128 + 128]
            if c % 4:
                tile = pltpu.roll(tile, 128 - 32 * (c % 4), 1)
            emsg[c, 0] = left
            emsg[c, 1] = tile.astype(BF16)

        def send_right(r, _):
            here = jnp.logical_and(r == me_r, dest_c == me_c)

            @pl.when(jnp.logical_not(here))
            def _():
                pltpu.make_async_remote_copy(
                    rmsg, rrecv.at[own_o % 6], r_send, r_recv, device_id=(r, dest_c), device_id_type=MESH
                ).start()

            @pl.when(here)
            def _():
                pltpu.make_async_copy(rmsg, rrecv.at[own_o % 6], r_recv).start()

            return 0

        lax.fori_loop(0, R_DEV, send_right, 0)

        def send_left(s, _):
            dst = (me_c + s) % C_DEV
            pltpu.make_async_remote_copy(
                emsg.at[dst], erecv.at[own_o], e_send, e_recv, device_id=(me_r, dst), device_id_type=MESH
            ).start()
            return 0

        lax.fori_loop(1, C_DEV, send_left, 0)
        pltpu.make_async_copy(emsg.at[me_c], erecv.at[own_o], e_recv).start()

    @pl.when(jnp.logical_not(is_owner))
    def _():
        c_out.wait()
        c_proj.wait()

    pltpu.make_async_copy(mid_v, mid_h, mid_sem).wait()
    pltpu.make_async_copy(msgs.at[0 : C_DEV - 1], msgs.at[0 : C_DEV - 1], s_send).wait()

    def sent_rows(i, _):
        @pl.when(col_of(block_y(i // 6), i % 6) != me_c)
        def _():
            pltpu.make_async_copy(wmsg.at[i], wmsg.at[i], w_send).wait()

        return 0

    lax.fori_loop(0, OWNERS, sent_rows, 0)

    pltpu.make_async_copy(rrecv, rrecv, r_recv).wait()
    right_o[...] = rrecv[...].astype(F32).reshape(NJ, 128)
    pltpu.make_async_copy(erecv, erecv, e_recv).wait()
    left_o[...] = erecv[:, 0].astype(F32).reshape(NI, 128)
    eye = jnp.where(iota((32, 128), 0) == iota((32, 128), 1), 1.0, 0.0).astype(BF16)
    seq_o[...] = nt(eye, erecv[:, 1].astype(F32).reshape(NI, 128).astype(BF16)).astype(BF16)

    @pl.when(is_owner)
    def _():
        pltpu.make_async_copy(emsg.at[0 : C_DEV - 1], emsg.at[0 : C_DEV - 1], e_send).wait()

        def sent_right(r, _):
            @pl.when(jnp.logical_not(jnp.logical_and(r == me_r, dest_c == me_c)))
            def _():
                pltpu.make_async_copy(rmsg, rmsg, r_send).wait()

            return 0

        lax.fori_loop(0, R_DEV, sent_right, 0)


def pair_kernel(mid_h, left_ref, right_ref, wpair_ref, out_h, mid_v, out_v, in_sem, out_sem):
    n = NI // KSTEPS

    def rows(k):
        return pl.ds(pl.multiple_of(k * n, n), n)

    def fetch(k):
        return pltpu.make_async_copy(mid_h.at[rows(k)], mid_v.at[rows(k)], in_sem.at[k])

    def put(k):
        return pltpu.make_async_copy(out_v.at[rows(k)], out_h.at[rows(k)], out_sem)

    for k in range(KSTEPS):
        fetch(k).start()
    lane = iota((NJ, C), 1)
    right = right_ref[...]
    scale = jnp.where(lane < 64, right, 1.0)
    shift = jnp.where(lane < 64, 0.0, -right)

    def step(k, _):
        fetch(k).wait()
        left = left_ref[rows(k), :].reshape(n, 1, C)
        feature = (left * scale[None] + shift[None]).astype(BF16).reshape(n * NJ, C)
        update = nn(feature, wpair_ref[...])
        mid = mid_v[rows(k)].astype(F32).reshape(n * NJ, C)
        out_v[rows(k)] = (mid + update).astype(BF16).reshape(n, NJ, C)
        put(k).start()
        return 0

    lax.fori_loop(0, KSTEPS, step, 0)
    pltpu.make_async_copy(out_v, out_h, out_sem).wait()


def local(pair, seq, w_hidden, w_back, w_bias, w_query, w_key, w_value, w_out, w_project, w_pair):
    hbm = pl.BlockSpec(memory_space=pl.ANY)
    vmem = pl.BlockSpec(memory_space=pltpu.VMEM)
    dma = pltpu.SemaphoreType.DMA
    mid, left, right, seq_new = pl.pallas_call(
        main_kernel,
        out_shape=(
            jax.ShapeDtypeStruct((NI, NJ, C), BF16),
            jax.ShapeDtypeStruct((NI, 128), F32),
            jax.ShapeDtypeStruct((NJ, 128), F32),
            jax.ShapeDtypeStruct((32, NI), BF16),
        ),
        in_specs=[hbm] * 10,
        out_specs=(hbm, vmem, vmem, vmem),
        scratch_shapes=[
            pltpu.VMEM((NI, NJ, C), BF16),
            pltpu.VMEM((NI, NJ, C), BF16),
            pltpu.VMEM((RC * NJ, C), BF16),
            pltpu.VMEM((RC * NJ, C), BF16),
            pltpu.VMEM((RC * NJ, C), BF16),
            pltpu.VMEM((RC * NJ, C), BF16),
            pltpu.VMEM((RC * NJ, C), F32),
            pltpu.VMEM((RC * NJ, C), F32),
            pltpu.VMEM((2, 6, NI, 128), F32),
            pltpu.VMEM((8 * C, 256), BF16),
            pltpu.VMEM((32, R_DEV * NI), BF16),
            pltpu.VMEM((C, PH), BF16),
            pltpu.VMEM((PH, C), BF16),
            pltpu.VMEM((HEADS, C), BF16),
            pltpu.VMEM((D, D), BF16),
            pltpu.VMEM((D, D), BF16),
            pltpu.VMEM((D, D), BF16),
            pltpu.VMEM((D, D), BF16),
            pltpu.VMEM((D, C), BF16),
            pltpu.VMEM((C_DEV, 32, 256), BF16),
            pltpu.VMEM((D, 256), BF16),
            pltpu.VMEM((D, 256), BF16),
            pltpu.VMEM((NI, D), BF16),
            pltpu.VMEM((NJ, 2 * D), F32),
            pltpu.VMEM((2, 16 * NJ, 512), BF16),
            pltpu.VMEM((2, 16 * NJ, 512), BF16),
            pltpu.VMEM((2, NI, 16 * NJ), BF16),
            pltpu.VMEM((256, D), BF16),
            pltpu.VMEM((OWNERS, OWN, WL), BF16),
            pltpu.VMEM((C_DEV, OWN, WL), BF16),
            pltpu.VMEM((C_DEV, 2, OWN, 128), BF16),
            pltpu.VMEM((OWNERS, 2, OWN, 128), BF16),
            pltpu.VMEM((OWN, 128), BF16),
            pltpu.VMEM((6, OWN, 128), BF16),
            dma((9,)),
            dma((STEPS,)),
            dma, dma, dma, dma, dma, dma, dma, dma, dma,
        ],
        compiler_params=pltpu.CompilerParams(
            collective_id=0, has_side_effects=True, vmem_limit_bytes=60 * 1024 * 1024
        ),
        name="trunk_main",
    )(pair, seq.T, w_hidden, w_back, w_bias.T, w_query, w_key, w_value, w_out, w_project)
    pair_out = pl.pallas_call(
        pair_kernel,
        out_shape=jax.ShapeDtypeStruct((NI, NJ, C), BF16),
        in_specs=[hbm, vmem, vmem, vmem],
        out_specs=hbm,
        scratch_shapes=[
            pltpu.VMEM((NI, NJ, C), BF16),
            pltpu.VMEM((NI, NJ, C), BF16),
            dma((KSTEPS,)),
            dma,
        ],
        compiler_params=pltpu.CompilerParams(vmem_limit_bytes=16 * 1024 * 1024),
        name="pair_update",
    )(mid, left, right, w_pair)
    return pair_out, seq_new.T


def solution(mesh):
    return jax.shard_map(
        local,
        mesh=mesh,
        in_specs=(P("row", "col", None), P(None, "col")) + (P(),) * 9,
        out_specs=(P("row", "col", None), P("row", "col")),
        check_vma=False,
    )
```

```python
import functools

import jax
import jax.numpy as jnp
from jax import lax
from jax.experimental import pallas as pl
from jax.experimental.pallas import tpu as pltpu
from jax.sharding import PartitionSpec as P

HEADS = 32
EPS = 1e-05
F32 = jnp.float32
BF16 = jnp.bfloat16

R_DEV, C_DEV = 8, 32
NI, NJ, C, D, PH = 192, 48, 128, 1024, 512
OWNERS, OWN = 24, 8
WL = D + 128
RC = 16
STEPS = NI // RC
BLK = 48
SPB = BLK // RC
KSTEPS = 4
SCALE = 32 ** (-0.5)
MESH = pl.DeviceIdType.MESH


def nt(a, b):
    return lax.dot_general(a, b, (((1,), (1,)), ((), ())), preferred_element_type=F32)


def tn(a, b):
    return lax.dot_general(a, b, (((0,), (0,)), ((), ())), preferred_element_type=F32)


def nn(a, b):
    return jnp.dot(a, b, preferred_element_type=F32)


def layer_norm(x, axis=-1):
    mean = jnp.mean(x, axis=axis, keepdims=True)
    cen = x - mean
    var = jnp.mean(cen * cen, axis=axis, keepdims=True)
    return cen * lax.rsqrt(var + EPS)


def iota(shape, dim):
    return lax.broadcasted_iota(jnp.int32, shape, dim)


def owner_of(col):
    y, x, z = lax.div(col, 8), lax.rem(lax.div(col, 2), 4), lax.rem(col, 2)
    xr = jnp.where(x > y, x - 1, x)
    return (y * 3 + xr) * 2 + z, x != y, y


def col_of(y, t):
    xr, z = (t // 2, t % 2) if isinstance(t, int) else (lax.div(t, 2), lax.rem(t, 2))
    x = jnp.where(xr >= y, xr + 1, xr)
    return (y * 4 + x) * 2 + z


def main_kernel(
    pair_h, seq_h, whid_h, wback_h, wbias_h, wq_h, wk_h, wv_h, wout_h, wproj_h,
    mid_h, left_o, right_o, seq_o,
    pair_v, mid_v, nb0, nb1, nb2, mb0, mb1, mb2, mn_v, bias_v, bmat_v,
    seq_v, whid_v, wback_v, wbias_v, wq_v, wk_v, wv_v, wout_v, wproj_v,
    msgs, sqk, raw_v, sqn, q_v, kv_v, kbd, vbd, w_v, expand_v, wmsg, wrecv, emsg, erecv, rmsg, rrecv,
    in_sem, pin_sem, mid_sem, s_send, s_recv, w_send, w_recv, e_send, e_recv, r_send, r_recv,
):
    me_r, me_c = lax.axis_index("row"), lax.axis_index("col")
    own_o, is_owner, me_y = owner_of(me_c)
    own_o = jnp.where(is_owner, own_o, 0)
    dest_c = 4 * me_r + me_y
    self_right = jnp.logical_and(is_owner, dest_c == me_c)

    def load(src, dst, k):
        cp = pltpu.make_async_copy(src, dst, in_sem.at[k])
        cp.start()
        return cp

    def block_y(cc):
        return lax.rem(me_y + 1 + cc, 4)

    def true_rows(k):
        if isinstance(k, int):
            return pl.ds(pl.multiple_of(block_y(k // SPB) * BLK + (k % SPB) * RC, RC), RC)
        return pl.ds(pl.multiple_of(block_y(lax.div(k, SPB)) * BLK + lax.rem(k, SPB) * RC, RC), RC)

    c_seq = load(seq_h, seq_v, 0)
    c_hid = load(whid_h, whid_v, 1)
    c_back = load(wback_h, wback_v, 2)
    c_bias = load(wbias_h, wbias_v, 3)

    def pair_copy(k):
        rows = pl.ds(pl.multiple_of(k * RC, RC), RC)
        return pltpu.make_async_copy(pair_h.at[true_rows(k)], pair_v.at[rows], pin_sem.at[k])

    for k in range(STEPS):
        pair_copy(k).start()
    c_q = load(wq_h, wq_v, 4)
    c_k = load(wk_h, wk_v, 5)
    c_v = load(wv_h, wv_v, 6)
    c_out = load(wout_h, wout_v, 7)
    c_proj = load(wproj_h, wproj_v, 8)

    barrier = pltpu.get_barrier_semaphore()
    src_r, src_y = lax.div(me_c, 4), lax.rem(me_c, 4)
    for t in range(6):
        src = col_of(src_y, t)

        @pl.when(jnp.logical_not(jnp.logical_and(src_r == me_r, src == me_c)))
        def _():
            pl.semaphore_signal(barrier, 1, device_id=(src_r, src), device_id_type=MESH)

    for s in range(1, C_DEV):
        pl.semaphore_signal(
            barrier, 1, device_id=(me_r, lax.rem(me_c + s, C_DEV)), device_id_type=MESH
        )

    c_seq.wait()
    lane32 = iota((32, 128), 1)
    base = pl.multiple_of((me_r * 3 // 2) * 128, 128)
    own = seq_v[:, pl.ds(base, 256)].astype(F32)
    own = jnp.where(me_r % 2 == 1, pltpu.roll(own, 192, 1), own)
    own0, own1 = own[:, 0:128].astype(BF16), own[:, 128:256]
    for c in range(C_DEV):
        t, o = (c * NJ) // 128, (c * NJ) % 128
        keys = seq_v[:, t * 128 : t * 128 + 128].astype(F32)
        if o + NJ > 128:
            keys = jnp.where(lane32 >= o, keys, seq_v[:, t * 128 + 128 : t * 128 + 256].astype(F32))
        if o != 64:
            keys = pltpu.roll(keys, (64 - o) % 128, 1)
        msgs[c, :, 0:128] = own0
        msgs[c, :, 128:256] = jnp.where(lane32 < 64, own1, jnp.where(lane32 < 112, keys, 0.0)).astype(BF16)

    c_bias.wait()
    spread = jnp.where(
        iota((32, 256), 0) == (iota((32, 256), 1) // 128) * 16 + iota((32, 256), 1) % 16, 1.0, 0.0
    ).astype(BF16)
    wide = tn(wbias_v[...], spread)
    slot = (iota((C, 256), 1) % 128) // 16
    for j8 in range(8):
        bmat_v[j8 * C : (j8 + 1) * C, :] = jnp.where(slot == j8, wide, 0.0).astype(BF16)
    head_lane = iota((128, D), 0) == iota((128, D), 1) // 32
    expand_v[0:128] = jnp.where(head_lane, 1.0, 0.0).astype(BF16)
    expand_v[128:256] = jnp.where(head_lane, 1.0, 0.0).astype(BF16)

    nb, mb = (nb0, nb1, nb2), (mb0, mb1, mb2)

    def rows_of(k):
        return pl.ds(pl.multiple_of(k * RC, RC), RC)

    def stage_norm(k, s):
        x = pair_v[rows_of(k)].astype(F32).reshape(RC * NJ, C)
        nb[s][...] = layer_norm(x).astype(BF16)

    def stage_hidden(k, s):
        hid = jnp.maximum(nn(nb[s][...], whid_v[...]), 0.0).astype(BF16)
        x = pair_v[rows_of(k)].astype(F32).reshape(RC * NJ, C)
        mid = (x + nn(hid, wback_v[...])).astype(BF16)
        mid_v[rows_of(k)] = mid.reshape(RC, NJ, C)
        mb[s][...] = mid

    def stage_mid(s):
        mn_v[s * RC * NJ : (s + 1) * RC * NJ] = layer_norm(mb[s][...].astype(F32))

    def stage_bias(b):
        blocks = []
        for jb in range(6):
            cols = []
            for j8 in range(8):
                j = jb * 8 + j8
                cols.append(
                    jnp.concatenate(
                        [mn_v[pl.ds(h * 8 * NJ + j, 8, stride=NJ), :] for h in range(BLK // 8)], axis=0
                    ).astype(BF16)
                )
            blocks.append(jnp.concatenate(cols, axis=1))
        out = nn(jnp.concatenate(blocks, axis=0), bmat_v[...])
        for jb in range(6):
            for g in range(2):
                bias_v[g, jb, pl.ds(pl.multiple_of(b * BLK, BLK), BLK), :] = out[
                    jb * BLK : (jb + 1) * BLK, g * 128 : (g + 1) * 128
                ]

    def mid_out(k):
        return pltpu.make_async_copy(mid_v.at[rows_of(k)], mid_h.at[true_rows(k)], mid_sem)

    def pair_block(t, _):
        for u in range(3):
            pair_copy(3 * t + 2 + u).wait()
        for u in range(3):
            k, s = 3 * t + 1 + u, (1 + u) % 3
            stage_hidden(k, s)
            stage_norm(k + 1, (s + 1) % 3)
            stage_mid(u)
        stage_bias(t)
        for u in range(3):
            mid_out(3 * t + u).start()
        return 0

    c_hid.wait()
    c_back.wait()
    pair_copy(0).wait()
    pair_copy(1).wait()
    pl.semaphore_wait(
        barrier, C_DEV - 1 + jnp.where(is_owner, R_DEV, 0) - jnp.where(self_right, 1, 0)
    )
    my_slab = pl.ds(pl.multiple_of(me_c * 32, 32), 32)
    for s in range(1, C_DEV):
        dst = lax.rem(me_c + s, C_DEV)
        pltpu.make_async_remote_copy(
            msgs.at[dst], sqk.at[my_slab], s_send, s_recv, device_id=(me_r, dst), device_id_type=MESH
        ).start()
    pltpu.make_async_copy(msgs.at[me_c], sqk.at[my_slab], s_recv).start()
    stage_norm(0, 0)
    stage_hidden(0, 0)
    stage_norm(1, 1)

    lax.fori_loop(0, 3, pair_block, 0)

    pltpu.make_async_copy(sqk, sqk, s_recv).wait()
    ident = jnp.where(iota((256, 256), 0) == iota((256, 256), 1), 1.0, 0.0).astype(BF16)
    raw_v[...] = nt(ident, sqk[...])

    def norm_rows(k, _):
        for u in range(4):
            rows = pl.ds(pl.multiple_of(k * 64 + u * 16, 16), 16)
            sqn[rows, :] = layer_norm(raw_v[rows, :]).astype(BF16)
        return 0

    lax.fori_loop(0, 4, norm_rows, 0)
    c_q.wait()
    q_v[...] = nn(sqn[:NI], wq_v[...]).astype(BF16)
    c_k.wait()
    c_v.wait()
    kv_v[:, 0:D] = nn(sqn[NI : NI + NJ], wk_v[...])
    kv_v[:, D : 2 * D] = nn(sqn[NI : NI + NJ], wv_v[...])
    head_here = iota((16, 512), 0) == iota((16, 512), 1) // 32

    def spread_keys(j4, _):
        for u in range(4):
            j = j4 * 4 + u
            dst = pl.ds(pl.multiple_of(j * 16, 16), 16)
            for g in range(2):
                krow = jnp.broadcast_to(kv_v[pl.ds(j, 1), g * 512 : (g + 1) * 512], (16, 512))
                vrow = jnp.broadcast_to(kv_v[pl.ds(j, 1), D + g * 512 : D + (g + 1) * 512], (16, 512))
                kbd[g, dst, :] = jnp.where(head_here, krow, 0.0).astype(BF16)
                vbd[g, dst, :] = jnp.where(head_here, vrow, 0.0).astype(BF16)
        return 0

    lax.fori_loop(0, NJ // 4, spread_keys, 0)

    def attend(first, count):
        n = count * BLK
        lane = iota((n, 128), 1)
        q = [
            q_v[pl.ds(pl.multiple_of(block_y(cc) * BLK, 16), BLK), :] for cc in range(first, first + count)
        ]
        q = q[0] if count == 1 else jnp.concatenate(q, axis=0)
        here = slice(first * BLK, first * BLK + n)
        parts = []
        for g in range(2):
            scores = nt(q[:, g * 512 : (g + 1) * 512], kbd[g])
            tiles = [scores[:, jb * 128 : (jb + 1) * 128] * SCALE + bias_v[g, jb, here, :] for jb in range(6)]
            top = functools.reduce(jnp.maximum, tiles)
            for shift in (16, 32, 64):
                top = jnp.maximum(top, pltpu.roll(top, shift, 1))
            total = None
            for jb in range(6):
                w = jnp.exp(tiles[jb] - top)
                w_v[g, here, jb * 128 : (jb + 1) * 128] = w.astype(BF16)
                total = w if total is None else total + w
            for shift in (16, 32, 64):
                total = total + pltpu.roll(total, shift, 1)
            weighted = nn(w_v[g, here, :], vbd[g])
            wmsg[first * 6 : (first + count) * 6, :, g * 512 : (g + 1) * 512] = weighted.reshape(
                count * 6, OWN, 512
            ).astype(BF16)
            high = top.astype(BF16).astype(F32)
            middle = (top - high).astype(BF16).astype(F32)
            low = (top - high) - middle
            parts.append((high, middle, low, total))
        stats = jnp.zeros((n, 128), F32)
        for p in range(4):
            for g in range(2):
                stats = jnp.where(lane // 16 == p * 2 + g, parts[g][p], stats)
        wmsg[first * 6 : (first + count) * 6, :, D:WL] = stats.reshape(count * 6, OWN, 128).astype(BF16)

        for i in range(count * 6):
            cc, t = first + i // 6, i % 6
            dst = col_of(block_y(cc), t)

            def start():
                pltpu.make_async_remote_copy(
                    wmsg.at[cc * 6 + t], wrecv.at[me_c], w_send, w_recv,
                    device_id=(me_r, dst), device_id_type=MESH,
                ).start()

            if cc < 3:
                start()
                continue
            mine = dst == me_c
            pl.when(jnp.logical_not(mine))(start)

            @pl.when(mine)
            def _():
                pltpu.make_async_copy(wmsg.at[cc * 6 + t], wrecv.at[me_c], w_recv).start()

    attend(0, 3)
    pair_copy(11).wait()
    stage_hidden(10, 1)
    stage_norm(11, 2)
    stage_mid(0)
    stage_hidden(11, 2)
    stage_mid(1)
    stage_mid(2)
    stage_bias(3)
    for k in range(9, 12):
        mid_out(k).start()
    attend(3, 1)

    @pl.when(is_owner)
    def _():
        resid = raw_v[pl.ds(pl.multiple_of(own_o * 8, 8), 8), :]
        c_out.wait()
        c_proj.wait()
        pltpu.make_async_copy(wrecv, wrecv, w_recv).wait()
        st = wrecv[:, :, D:WL].astype(F32).reshape(C_DEV * OWN, 128)
        m = (st + pltpu.roll(st, 96, 1)) + pltpu.roll(st, 64, 1)
        den = pltpu.roll(st, 32, 1)
        m3 = m.reshape(C_DEV, OWN, 128)
        top = jnp.max(m3, axis=0)
        fac = jnp.where(iota((C_DEV, OWN, 128), 2) < 32, jnp.exp(jnp.minimum(m3 - top[None], 0.0)), 0.0)
        whole = jnp.sum(fac * den.reshape(C_DEV, OWN, 128), axis=0)
        whole = jnp.where(iota((OWN, 128), 1) < 32, whole, 1.0)
        fac = (fac / whole[None]).reshape(C_DEV * OWN, 128)
        high = fac.astype(BF16)
        low = (fac - high.astype(F32)).astype(BF16)
        wide = nn(jnp.concatenate([high, low], axis=1), expand_v[...]).reshape(C_DEV, OWN, D)
        attended = jnp.sum(wide * wrecv[:, :, 0:D].astype(F32), axis=0).astype(BF16)
        seq_new = (resid + nn(attended, wout_v[...])).astype(BF16).astype(F32)
        proj = nn(layer_norm(seq_new).astype(BF16), wproj_v[...]).astype(BF16).astype(F32)
        turned = pltpu.roll(proj, 64, 1)
        lane8 = iota((OWN, 128), 1)
        left = jnp.where(lane8 < 64, proj, turned).astype(BF16)
        right = jnp.where(lane8 < 64, turned, proj).astype(BF16)
        rmsg[...] = right
        for c in range(C_DEV):
            tile = seq_new[:, (c // 4) * 128 : (c // 4) * 128 + 128]
            if c % 4:
                tile = pltpu.roll(tile, 128 - 32 * (c % 4), 1)
            emsg[c, 0] = left
            emsg[c, 1] = tile.astype(BF16)

        slot = lax.rem(own_o, 6)
        for r in range(R_DEV):
            here = jnp.logical_and(r == me_r, dest_c == me_c)

            @pl.when(jnp.logical_not(here))
            def _():
                pltpu.make_async_remote_copy(
                    rmsg, rrecv.at[slot], r_send, r_recv, device_id=(r, dest_c), device_id_type=MESH
                ).start()

            @pl.when(here)
            def _():
                pltpu.make_async_copy(rmsg, rrecv.at[slot], r_recv).start()

        for s in range(1, C_DEV):
            dst = lax.rem(me_c + (s + 15) % 31 + 1, C_DEV)
            pltpu.make_async_remote_copy(
                emsg.at[dst], erecv.at[own_o], e_send, e_recv, device_id=(me_r, dst), device_id_type=MESH
            ).start()
        pltpu.make_async_copy(emsg.at[me_c], erecv.at[own_o], e_recv).start()

    @pl.when(jnp.logical_not(is_owner))
    def _():
        c_out.wait()
        c_proj.wait()

    pltpu.make_async_copy(mid_v, mid_h, mid_sem).wait()
    pltpu.make_async_copy(msgs.at[0 : C_DEV - 1], msgs.at[0 : C_DEV - 1], s_send).wait()

    def sent_rows(i, _):
        @pl.when(col_of(block_y(lax.div(i, 6)), lax.rem(i, 6)) != me_c)
        def _():
            pltpu.make_async_copy(wmsg.at[i], wmsg.at[i], w_send).wait()

        return 0

    lax.fori_loop(0, OWNERS, sent_rows, 0)

    pltpu.make_async_copy(rrecv, rrecv, r_recv).wait()
    right_o[...] = rrecv[...].astype(F32).reshape(NJ, 128)
    pltpu.make_async_copy(erecv, erecv, e_recv).wait()
    left_o[...] = erecv[:, 0].astype(F32).reshape(NI, 128)
    eye = jnp.where(iota((32, 128), 0) == iota((32, 128), 1), 1.0, 0.0).astype(BF16)
    seq_o[...] = nt(eye, erecv[:, 1].astype(F32).reshape(NI, 128).astype(BF16)).astype(BF16)

    @pl.when(is_owner)
    def _():
        pltpu.make_async_copy(emsg.at[0 : C_DEV - 1], emsg.at[0 : C_DEV - 1], e_send).wait()

        def sent_right(r, _):
            @pl.when(jnp.logical_not(jnp.logical_and(r == me_r, dest_c == me_c)))
            def _():
                pltpu.make_async_copy(rmsg, rmsg, r_send).wait()

            return 0

        lax.fori_loop(0, R_DEV, sent_right, 0)


def pair_kernel(
    mid_h, left_h, right_h, wpair_h, seqt_h, out_h, seq_o,
    left_ref, right_ref, wpair_ref, seq_v, mid_v, out_v, small_sem, in_sem, out_sem,
):
    n = NI // KSTEPS

    def rows(k):
        return pl.ds(pl.multiple_of(k * n, n), n)

    def fetch(k):
        return pltpu.make_async_copy(mid_h.at[rows(k)], mid_v.at[rows(k)], in_sem.at[k])

    def put(k):
        return pltpu.make_async_copy(out_v.at[rows(k)], out_h.at[rows(k)], out_sem)

    small = [
        pltpu.make_async_copy(left_h, left_ref, small_sem.at[0]),
        pltpu.make_async_copy(right_h, right_ref, small_sem.at[1]),
        pltpu.make_async_copy(wpair_h, wpair_ref, small_sem.at[2]),
        pltpu.make_async_copy(seqt_h, seq_v, small_sem.at[3]),
    ]
    for cp in small:
        cp.start()
    for k in range(KSTEPS):
        fetch(k).start()
    for cp in small:
        cp.wait()
    seq_put = pltpu.make_async_copy(seq_v, seq_o, small_sem.at[0])
    seq_put.start()
    lane = iota((NJ, C), 1)
    right = right_ref[...]
    scale = jnp.where(lane < 64, right, 1.0)
    shift = jnp.where(lane < 64, 0.0, -right)

    def step(k, _):
        fetch(k).wait()
        left = left_ref[rows(k), :].reshape(n, 1, C)
        feature = (left * scale[None] + shift[None]).astype(BF16).reshape(n * NJ, C)
        update = nn(feature, wpair_ref[...])
        mid = mid_v[rows(k)].astype(F32).reshape(n * NJ, C)
        out_v[rows(k)] = (mid + update).astype(BF16).reshape(n, NJ, C)
        put(k).start()
        return 0

    lax.fori_loop(0, KSTEPS, step, 0)
    seq_put.wait()
    pltpu.make_async_copy(out_v, out_h, out_sem).wait()


def local(pair, seq, w_hidden, w_back, w_bias, w_query, w_key, w_value, w_out, w_project, w_pair):
    hbm = pl.BlockSpec(memory_space=pl.ANY)
    vmem = pl.BlockSpec(memory_space=pltpu.VMEM)
    dma = pltpu.SemaphoreType.DMA
    mid, left, right, seq_new = pl.pallas_call(
        main_kernel,
        out_shape=(
            jax.ShapeDtypeStruct((NI, NJ, C), BF16),
            jax.ShapeDtypeStruct((NI, 128), F32),
            jax.ShapeDtypeStruct((NJ, 128), F32),
            jax.ShapeDtypeStruct((32, NI), BF16),
        ),
        in_specs=[hbm] * 10,
        out_specs=(hbm, vmem, vmem, vmem),
        scratch_shapes=[
            pltpu.VMEM((NI, NJ, C), BF16),
            pltpu.VMEM((NI, NJ, C), BF16),
            pltpu.VMEM((RC * NJ, C), BF16),
            pltpu.VMEM((RC * NJ, C), BF16),
            pltpu.VMEM((RC * NJ, C), BF16),
            pltpu.VMEM((RC * NJ, C), BF16),
            pltpu.VMEM((RC * NJ, C), BF16),
            pltpu.VMEM((RC * NJ, C), BF16),
            pltpu.VMEM((BLK * NJ, C), F32),
            pltpu.VMEM((2, 6, NI, 128), F32),
            pltpu.VMEM((8 * C, 256), BF16),
            pltpu.VMEM((32, R_DEV * NI), BF16),
            pltpu.VMEM((C, PH), BF16),
            pltpu.VMEM((PH, C), BF16),
            pltpu.VMEM((HEADS, C), BF16),
            pltpu.VMEM((D, D), BF16),
            pltpu.VMEM((D, D), BF16),
            pltpu.VMEM((D, D), BF16),
            pltpu.VMEM((D, D), BF16),
            pltpu.VMEM((D, C), BF16),
            pltpu.VMEM((C_DEV, 32, 256), BF16),
            pltpu.VMEM((D, 256), BF16),
            pltpu.VMEM((256, D), F32),
            pltpu.VMEM((256, D), BF16),
            pltpu.VMEM((NI, D), BF16),
            pltpu.VMEM((NJ, 2 * D), F32),
            pltpu.VMEM((2, 16 * NJ, 512), BF16),
            pltpu.VMEM((2, 16 * NJ, 512), BF16),
            pltpu.VMEM((2, NI, 16 * NJ), BF16),
            pltpu.VMEM((256, D), BF16),
            pltpu.VMEM((OWNERS, OWN, WL), BF16),
            pltpu.VMEM((C_DEV, OWN, WL), BF16),
            pltpu.VMEM((C_DEV, 2, OWN, 128), BF16),
            pltpu.VMEM((OWNERS, 2, OWN, 128), BF16),
            pltpu.VMEM((OWN, 128), BF16),
            pltpu.VMEM((6, OWN, 128), BF16),
            dma((9,)),
            dma((STEPS,)),
            dma, dma, dma, dma, dma, dma, dma, dma, dma,
        ],
        compiler_params=pltpu.CompilerParams(
            collective_id=0, has_side_effects=True, vmem_limit_bytes=60 * 1024 * 1024
        ),
        name="trunk_main",
    )(pair, seq.T, w_hidden, w_back, w_bias.T, w_query, w_key, w_value, w_out, w_project)
    pair_out, seq_out = pl.pallas_call(
        pair_kernel,
        out_shape=(jax.ShapeDtypeStruct((NI, NJ, C), BF16), jax.ShapeDtypeStruct((32, NI), BF16)),
        in_specs=[hbm] * 5,
        out_specs=(hbm, hbm),
        scratch_shapes=[
            pltpu.VMEM((NI, 128), F32),
            pltpu.VMEM((NJ, 128), F32),
            pltpu.VMEM((C, C), BF16),
            pltpu.VMEM((32, NI), BF16),
            pltpu.VMEM((NI, NJ, C), BF16),
            pltpu.VMEM((NI, NJ, C), BF16),
            dma((4,)),
            dma((KSTEPS,)),
            dma,
        ],
        compiler_params=pltpu.CompilerParams(vmem_limit_bytes=60 * 1024 * 1024),
        name="pair_update",
    )(mid, left, right, w_pair, seq_new)
    return pair_out, seq_out.T


def solution(mesh):
    return jax.shard_map(
        local,
        mesh=mesh,
        in_specs=(P("row", "col", None), P(None, "col")) + (P(),) * 9,
        out_specs=(P("row", "col", None), P("row", "col")),
        check_vma=False,
    )
```

```python
import functools

import jax
import jax.numpy as jnp
from jax import lax
from jax.experimental import pallas as pl
from jax.experimental.pallas import tpu as pltpu
from jax.sharding import PartitionSpec as P

HEADS = 32
EPS = 1e-05
F32 = jnp.float32
BF16 = jnp.bfloat16

R_DEV, C_DEV = 8, 32
NI, NJ, C, D, PH = 192, 48, 128, 1024, 512
OWNERS, OWN = 24, 8
WL = D + 128
RC = 16
STEPS = NI // RC
BLK = 48
SPB = BLK // RC
KSTEPS = 4
KROWS = NI // KSTEPS
SCALE = 32 ** (-0.5)
MESH = pl.DeviceIdType.MESH


def nt(a, b):
    return lax.dot_general(a, b, (((1,), (1,)), ((), ())), preferred_element_type=F32)


def tn(a, b):
    return lax.dot_general(a, b, (((0,), (0,)), ((), ())), preferred_element_type=F32)


def nn(a, b):
    return jnp.dot(a, b, preferred_element_type=F32)


def layer_norm(x, axis=-1):
    mean = jnp.mean(x, axis=axis, keepdims=True)
    cen = x - mean
    var = jnp.mean(cen * cen, axis=axis, keepdims=True)
    return cen * lax.rsqrt(var + EPS)


def row_sum(x):
    parts = [x[:, t : t + 128] for t in range(0, D, 128)]
    while len(parts) > 1:
        parts = [a + b for a, b in zip(parts[0::2], parts[1::2])]
    return jnp.sum(parts[0], axis=-1, keepdims=True)


def wide_norm(x):
    cen = x - row_sum(x) * (1.0 / D)
    return cen * lax.rsqrt(row_sum(cen * cen) * (1.0 / D) + EPS)


def iota(shape, dim):
    return lax.broadcasted_iota(jnp.int32, shape, dim)


def owner_of(col):
    y, x, z = lax.div(col, 8), lax.rem(lax.div(col, 2), 4), lax.rem(col, 2)
    xr = jnp.where(x > y, x - 1, x)
    return (y * 3 + xr) * 2 + z, x != y, y


def col_of(y, t):
    xr, z = (t // 2, t % 2) if isinstance(t, int) else (lax.div(t, 2), lax.rem(t, 2))
    x = jnp.where(xr >= y, xr + 1, xr)
    return (y * 4 + x) * 2 + z


def main_kernel(
    pair_h, seq_h, whid_h, wback_h, wbias_h, wq_h, wk_h, wv_h, wout_h, wproj_h,
    mid_h, left_o, right_o,
    pair_v, mid_v, nb0, nb1, nb2, mb0, mb1, mb2, mn_v, bias_v, bmat_v,
    seq_v, whid_v, wback_v, wbias_v, wq_v, wk_v, wv_v, wout_v, wproj_v,
    own0_v, msgs, sqk0, sqk1, raw_v, sqn, q_v, kv_v, kbd, vbd, w_v, expand_v, wmsg, wrecv, emsg, erecv, rmsg, rrecv,
    in_sem, pin_sem, mid_sem, s0_send, s0_recv, s1_send, s1_recv, w_send, w_recv, e_send, e_recv, r_send, r_recv,
):
    me_r, me_c = lax.axis_index("row"), lax.axis_index("col")
    own_o, is_owner, me_y = owner_of(me_c)
    own_o = jnp.where(is_owner, own_o, 0)
    dest_c = 4 * me_r + me_y
    self_right = jnp.logical_and(is_owner, dest_c == me_c)

    def load(src, dst, k):
        cp = pltpu.make_async_copy(src, dst, in_sem.at[k])
        cp.start()
        return cp

    def block_y(cc):
        return lax.rem(me_y + 1 + cc, 4)

    def true_rows(k):
        if isinstance(k, int):
            return pl.ds(pl.multiple_of(block_y(k // SPB) * BLK + (k % SPB) * RC, RC), RC)
        return pl.ds(pl.multiple_of(block_y(lax.div(k, SPB)) * BLK + lax.rem(k, SPB) * RC, RC), RC)

    c_seq = load(seq_h, seq_v, 0)
    c_hid = load(whid_h, whid_v, 1)
    c_back = load(wback_h, wback_v, 2)
    c_bias = load(wbias_h, wbias_v, 3)

    def pair_copy(k):
        rows = pl.ds(pl.multiple_of(k * RC, RC), RC)
        return pltpu.make_async_copy(pair_h.at[true_rows(k)], pair_v.at[rows], pin_sem.at[k])

    for k in range(STEPS):
        pair_copy(k).start()
    c_q = load(wq_h, wq_v, 4)
    c_k = load(wk_h, wk_v, 5)
    c_v = load(wv_h, wv_v, 6)
    c_out = load(wout_h, wout_v, 7)
    c_proj = load(wproj_h, wproj_v, 8)

    barrier = pltpu.get_barrier_semaphore()
    src_r, src_y = lax.div(me_c, 4), lax.rem(me_c, 4)
    for t in range(6):
        src = col_of(src_y, t)

        @pl.when(jnp.logical_not(jnp.logical_and(src_r == me_r, src == me_c)))
        def _():
            pl.semaphore_signal(barrier, 1, device_id=(src_r, src), device_id_type=MESH)

    for s in range(1, C_DEV):
        pl.semaphore_signal(
            barrier, 1, device_id=(me_r, lax.rem(me_c + s, C_DEV)), device_id_type=MESH
        )

    c_seq.wait()
    lane32 = iota((32, 128), 1)
    base = pl.multiple_of((me_r * 3 // 2) * 128, 128)
    own = seq_v[:, pl.ds(base, 256)].astype(F32)
    own = jnp.where(me_r % 2 == 1, pltpu.roll(own, 192, 1), own)
    own0_v[...] = own[:, 0:128].astype(BF16)
    own1 = own[:, 128:256]
    for c in range(C_DEV):
        t, o = (c * NJ) // 128, (c * NJ) % 128
        keys = seq_v[:, t * 128 : t * 128 + 128].astype(F32)
        if o + NJ > 128:
            keys = jnp.where(lane32 >= o, keys, seq_v[:, t * 128 + 128 : t * 128 + 256].astype(F32))
        if o != 64:
            keys = pltpu.roll(keys, (64 - o) % 128, 1)
        msgs[c] = jnp.where(lane32 < 64, own1, jnp.where(lane32 < 112, keys, 0.0)).astype(BF16)

    pl.semaphore_wait(
        barrier, C_DEV - 1 + jnp.where(is_owner, R_DEV, 0) - jnp.where(self_right, 1, 0)
    )
    my_slab = pl.ds(pl.multiple_of(me_c * 32, 32), 32)
    for s in range(1, C_DEV):
        dst = lax.rem(me_c + s, C_DEV)
        pltpu.make_async_remote_copy(
            msgs.at[dst], sqk1.at[my_slab], s1_send, s1_recv, device_id=(me_r, dst), device_id_type=MESH
        ).start()
    for s in range(1, C_DEV):
        dst = lax.rem(me_c + s, C_DEV)
        pltpu.make_async_remote_copy(
            own0_v, sqk0.at[my_slab], s0_send, s0_recv, device_id=(me_r, dst), device_id_type=MESH
        ).start()
    pltpu.make_async_copy(msgs.at[me_c], sqk1.at[my_slab], s1_recv).start()
    pltpu.make_async_copy(own0_v, sqk0.at[my_slab], s0_recv).start()

    c_bias.wait()
    spread = jnp.where(
        iota((32, 256), 0) == (iota((32, 256), 1) // 128) * 16 + iota((32, 256), 1) % 16, 1.0, 0.0
    ).astype(BF16)
    wide = tn(wbias_v[...], spread)
    slot = (iota((C, 256), 1) % 128) // 16
    for j8 in range(8):
        bmat_v[j8 * C : (j8 + 1) * C, :] = jnp.where(slot == j8, wide, 0.0).astype(BF16)
    head_lane = iota((128, D), 0) == iota((128, D), 1) // 32
    expand_v[0:128] = jnp.where(head_lane, 1.0, 0.0).astype(BF16)
    expand_v[128:256] = jnp.where(head_lane, 1.0, 0.0).astype(BF16)

    nb, mb = (nb0, nb1, nb2), (mb0, mb1, mb2)

    def rows_of(k):
        return pl.ds(pl.multiple_of(k * RC, RC), RC)

    def stage_norm(k, s):
        x = pair_v[rows_of(k)].astype(F32).reshape(RC * NJ, C)
        nb[s][...] = layer_norm(x).astype(BF16)

    def stage_hidden(k, s):
        hid = jnp.maximum(nn(nb[s][...], whid_v[...]), 0.0).astype(BF16)
        x = pair_v[rows_of(k)].astype(F32).reshape(RC * NJ, C)
        mid = (x + nn(hid, wback_v[...])).astype(BF16)
        mid_v[rows_of(k)] = mid.reshape(RC, NJ, C)
        mb[s][...] = mid

    def stage_mid(s):
        mn_v[s * RC * NJ : (s + 1) * RC * NJ] = layer_norm(mb[s][...].astype(F32))

    def stage_bias(b):
        blocks = []
        for jb in range(6):
            cols = []
            for j8 in range(8):
                j = jb * 8 + j8
                cols.append(
                    jnp.concatenate(
                        [mn_v[pl.ds(h * 8 * NJ + j, 8, stride=NJ), :] for h in range(BLK // 8)], axis=0
                    ).astype(BF16)
                )
            blocks.append(jnp.concatenate(cols, axis=1))
        out = nn(jnp.concatenate(blocks, axis=0), bmat_v[...])
        for jb in range(6):
            for g in range(2):
                bias_v[g, jb, pl.ds(pl.multiple_of(b * BLK, BLK), BLK), :] = out[
                    jb * BLK : (jb + 1) * BLK, g * 128 : (g + 1) * 128
                ]

    def mid_out(k):
        return pltpu.make_async_copy(mid_v.at[rows_of(k)], mid_h.at[true_rows(k)], mid_sem)

    def pair_block(t, _, first=False):
        for u in range(3):
            pair_copy(3 * t + 2 + u).wait()
        if first:
            stage_norm(0, 0)
            stage_hidden(0, 0)
            stage_norm(1, 1)
        else:
            stage_bias(t - 1)
        for u in range(3):
            k, s = 3 * t + 1 + u, (1 + u) % 3
            stage_hidden(k, s)
            stage_norm(k + 1, (s + 1) % 3)
            stage_mid(u)
        for u in range(3):
            mid_out(3 * t + u).start()
        return 0

    c_hid.wait()
    c_back.wait()
    pair_copy(0).wait()
    pair_copy(1).wait()
    pair_block(0, 0, first=True)
    lax.fori_loop(1, 3, pair_block, 0)
    stage_bias(2)

    ident = jnp.where(iota((128, 128), 0) == iota((128, 128), 1), 1.0, 0.0).astype(BF16)

    def norm_rows(k, _):
        for u in range(4):
            rows = pl.ds(pl.multiple_of(k * 64 + u * 16, 16), 16)
            sqn[rows, :] = wide_norm(raw_v[rows, :]).astype(BF16)
        return 0

    pltpu.make_async_copy(sqk1, sqk1, s1_recv).wait()
    raw_v[128:256] = nt(ident, sqk1[...])
    lax.fori_loop(2, 4, norm_rows, 0)
    c_k.wait()
    c_v.wait()
    kv_v[:, 0:D] = nn(sqn[NI : NI + NJ], wk_v[...])
    kv_v[:, D : 2 * D] = nn(sqn[NI : NI + NJ], wv_v[...])
    head_here = iota((16, 512), 0) == iota((16, 512), 1) // 32

    def spread_keys(j4, _):
        for u in range(4):
            j = j4 * 4 + u
            dst = pl.ds(pl.multiple_of(j * 16, 16), 16)
            for g in range(2):
                krow = jnp.broadcast_to(kv_v[pl.ds(j, 1), g * 512 : (g + 1) * 512], (16, 512))
                vrow = jnp.broadcast_to(kv_v[pl.ds(j, 1), D + g * 512 : D + (g + 1) * 512], (16, 512))
                kbd[g, dst, :] = jnp.where(head_here, krow, 0.0).astype(BF16)
                vbd[g, dst, :] = jnp.where(head_here, vrow, 0.0).astype(BF16)
        return 0

    lax.fori_loop(0, NJ // 4, spread_keys, 0)
    pltpu.make_async_copy(sqk0, sqk0, s0_recv).wait()
    raw_v[0:128] = nt(ident, sqk0[...])
    lax.fori_loop(0, 2, norm_rows, 0)
    c_q.wait()
    q_v[...] = nn(sqn[:NI], wq_v[...]).astype(BF16)

    def attend(first, count):
        n = count * BLK
        lane = iota((n, 128), 1)
        q = [
            q_v[pl.ds(pl.multiple_of(block_y(cc) * BLK, 16), BLK), :] for cc in range(first, first + count)
        ]
        q = q[0] if count == 1 else jnp.concatenate(q, axis=0)
        here = slice(first * BLK, first * BLK + n)
        parts = []
        for g in range(2):
            scores = nt(q[:, g * 512 : (g + 1) * 512], kbd[g])
            tiles = [scores[:, jb * 128 : (jb + 1) * 128] * SCALE + bias_v[g, jb, here, :] for jb in range(6)]
            top = functools.reduce(jnp.maximum, tiles)
            for shift in (16, 32, 64):
                top = jnp.maximum(top, pltpu.roll(top, shift, 1))
            total = None
            for jb in range(6):
                w = jnp.exp(tiles[jb] - top)
                w_v[g, here, jb * 128 : (jb + 1) * 128] = w.astype(BF16)
                total = w if total is None else total + w
            for shift in (16, 32, 64):
                total = total + pltpu.roll(total, shift, 1)
            weighted = nn(w_v[g, here, :], vbd[g])
            wmsg[first * 6 : (first + count) * 6, :, g * 512 : (g + 1) * 512] = weighted.reshape(
                count * 6, OWN, 512
            ).astype(BF16)
            high = top.astype(BF16).astype(F32)
            middle = (top - high).astype(BF16).astype(F32)
            low = (top - high) - middle
            parts.append((high, middle, low, total))
        stats = jnp.zeros((n, 128), F32)
        for p in range(4):
            for g in range(2):
                stats = jnp.where(lane // 16 == p * 2 + g, parts[g][p], stats)
        wmsg[first * 6 : (first + count) * 6, :, D:WL] = stats.reshape(count * 6, OWN, 128).astype(BF16)

        for i in range(count * 6):
            cc, t = first + i // 6, i % 6
            dst = col_of(block_y(cc), t)

            def start():
                pltpu.make_async_remote_copy(
                    wmsg.at[cc * 6 + t], wrecv.at[me_c], w_send, w_recv,
                    device_id=(me_r, dst), device_id_type=MESH,
                ).start()

            if cc < 3:
                start()
                continue
            mine = dst == me_c
            pl.when(jnp.logical_not(mine))(start)

            @pl.when(mine)
            def _():
                pltpu.make_async_copy(wmsg.at[cc * 6 + t], wrecv.at[me_c], w_recv).start()

    attend(0, 3)
    pair_copy(11).wait()
    stage_hidden(10, 1)
    stage_norm(11, 2)
    stage_mid(0)
    stage_hidden(11, 2)
    stage_mid(1)
    stage_mid(2)
    stage_bias(3)
    for k in range(9, 12):
        mid_out(k).start()
    attend(3, 1)

    @pl.when(is_owner)
    def _():
        resid = raw_v[pl.ds(pl.multiple_of(own_o * 8, 8), 8), :]
        c_out.wait()
        c_proj.wait()
        pltpu.make_async_copy(wrecv, wrecv, w_recv).wait()
        st = wrecv[:, :, D:WL].astype(F32).reshape(C_DEV * OWN, 128)
        m = (st + pltpu.roll(st, 96, 1)) + pltpu.roll(st, 64, 1)
        den = pltpu.roll(st, 32, 1)
        m3 = m.reshape(C_DEV, OWN, 128)
        top = jnp.max(m3, axis=0)
        fac = jnp.where(iota((C_DEV, OWN, 128), 2) < 32, jnp.exp(jnp.minimum(m3 - top[None], 0.0)), 0.0)
        whole = jnp.sum(fac * den.reshape(C_DEV, OWN, 128), axis=0)
        whole = jnp.where(iota((OWN, 128), 1) < 32, whole, 1.0)
        fac = (fac / whole[None]).reshape(C_DEV * OWN, 128)
        high = fac.astype(BF16)
        low = (fac - high.astype(F32)).astype(BF16)
        wide = nn(jnp.concatenate([high, low], axis=1), expand_v[...]).reshape(C_DEV, OWN, D)
        attended = jnp.sum(wide * wrecv[:, :, 0:D].astype(F32), axis=0).astype(BF16)
        seq_new = (resid + nn(attended, wout_v[...])).astype(BF16).astype(F32)
        proj = nn(wide_norm(seq_new).astype(BF16), wproj_v[...]).astype(BF16).astype(F32)
        turned = pltpu.roll(proj, 64, 1)
        lane8 = iota((OWN, 128), 1)
        right = jnp.where(lane8 < 64, turned, proj).astype(BF16)
        rmsg[...] = right
        for c in range(C_DEV):
            tile = seq_new[:, (c // 4) * 128 : (c // 4) * 128 + 128]
            if c % 4 != 2:
                tile = pltpu.roll(tile, (192 - 32 * (c % 4)) % 128, 1)
            emsg[c] = jnp.where(lane8 < 64, proj, tile).astype(BF16)

        slot = lax.rem(own_o, 6)
        for r in range(R_DEV):
            here = jnp.logical_and(r == me_r, dest_c == me_c)

            @pl.when(jnp.logical_not(here))
            def _():
                pltpu.make_async_remote_copy(
                    rmsg, rrecv.at[slot], r_send, r_recv, device_id=(r, dest_c), device_id_type=MESH
                ).start()

            @pl.when(here)
            def _():
                pltpu.make_async_copy(rmsg, rrecv.at[slot], r_recv).start()

        for s in range(1, C_DEV):
            dst = lax.rem(me_c + (s + 15) % 31 + 1, C_DEV)
            pltpu.make_async_remote_copy(
                emsg.at[dst], erecv.at[own_o], e_send, e_recv, device_id=(me_r, dst), device_id_type=MESH
            ).start()
        pltpu.make_async_copy(emsg.at[me_c], erecv.at[own_o], e_recv).start()

    @pl.when(jnp.logical_not(is_owner))
    def _():
        c_out.wait()
        c_proj.wait()

    pltpu.make_async_copy(mid_v, mid_h, mid_sem).wait()
    pltpu.make_async_copy(msgs.at[0 : C_DEV - 1], msgs.at[0 : C_DEV - 1], s1_send).wait()
    others = pl.ds(0, 32 * (C_DEV - 1))
    pltpu.make_async_copy(sqk0.at[others], sqk0.at[others], s0_send).wait()

    def sent_rows(i, _):
        @pl.when(col_of(block_y(lax.div(i, 6)), lax.rem(i, 6)) != me_c)
        def _():
            pltpu.make_async_copy(wmsg.at[i], wmsg.at[i], w_send).wait()

        return 0

    lax.fori_loop(0, OWNERS, sent_rows, 0)

    pltpu.make_async_copy(rrecv, rrecv, r_recv).wait()
    right_put = pltpu.make_async_copy(rrecv, right_o, in_sem.at[0])
    right_put.start()
    pltpu.make_async_copy(erecv, erecv, e_recv).wait()
    left_put = pltpu.make_async_copy(erecv, left_o, in_sem.at[1])
    left_put.start()

    @pl.when(is_owner)
    def _():
        pltpu.make_async_copy(emsg.at[0 : C_DEV - 1], emsg.at[0 : C_DEV - 1], e_send).wait()

        def sent_right(r, _):
            @pl.when(jnp.logical_not(jnp.logical_and(r == me_r, dest_c == me_c)))
            def _():
                pltpu.make_async_copy(rmsg, rmsg, r_send).wait()

            return 0

        lax.fori_loop(0, R_DEV, sent_right, 0)
    right_put.wait()
    left_put.wait()


def pair_kernel(
    mid_h, left_h, right_h, wpair_h, out_h, seq_h,
    left_b, right_b, wpair_v, left_v, seq_v, mid_v, out_v, small_sem, in_sem, out_sem,
):
    spans = [pl.ds(k * KROWS, KROWS) for k in range(KSTEPS)]
    small = [
        pltpu.make_async_copy(src, dst, small_sem.at[k])
        for k, (src, dst) in enumerate(((left_h, left_b), (right_h, right_b), (wpair_h, wpair_v)))
    ]
    for cp in small:
        cp.start()
    fetches = [pltpu.make_async_copy(mid_h.at[r], mid_v.at[r], in_sem.at[k]) for k, r in enumerate(spans)]
    for cp in fetches:
        cp.start()
    for cp in small:
        cp.wait()
    lane = iota((NJ, C), 1)
    right = right_b[...].astype(F32).reshape(NJ, C)
    scale = jnp.where(lane < 64, right, 1.0)
    shift = jnp.where(lane < 64, 0.0, -right)
    arrived = left_b[...].astype(F32).reshape(NI, C)
    left_v[...] = jnp.where(iota((NI, C), 1) < 64, arrived, pltpu.roll(arrived, 64, 1))
    pick = jnp.where(iota((32, C), 1) == iota((32, C), 0) + 64, 1.0, 0.0).astype(BF16)
    seq_v[...] = nt(pick, left_b[...].reshape(NI, C)).astype(BF16)
    seq_put = pltpu.make_async_copy(seq_v, seq_h, small_sem.at[0])
    seq_put.start()

    def step(k, _):
        rows = pl.ds(pl.multiple_of(k * KROWS, KROWS), KROWS)
        pltpu.make_async_copy(mid_h.at[rows], mid_v.at[rows], in_sem.at[k]).wait()
        left = left_v[rows, :].reshape(KROWS, 1, C)
        feature = (left * scale[None] + shift[None]).astype(BF16).reshape(KROWS * NJ, C)
        update = nn(feature, wpair_v[...])
        mid = mid_v[rows].astype(F32).reshape(KROWS * NJ, C)
        out_v[rows] = (mid + update).astype(BF16).reshape(KROWS, NJ, C)
        pltpu.make_async_copy(out_v.at[rows], out_h.at[rows], out_sem).start()
        return 0

    lax.fori_loop(0, KSTEPS, step, 0)
    seq_put.wait()
    pltpu.make_async_copy(out_v, out_h, out_sem).wait()


def local(pair, seq, w_hidden, w_back, w_bias, w_query, w_key, w_value, w_out, w_project, w_pair):
    hbm = pl.BlockSpec(memory_space=pl.ANY)
    dma = pltpu.SemaphoreType.DMA
    mid, left, right = pl.pallas_call(
        main_kernel,
        out_shape=(
            jax.ShapeDtypeStruct((NI, NJ, C), BF16),
            jax.ShapeDtypeStruct((OWNERS, OWN, 128), BF16),
            jax.ShapeDtypeStruct((6, OWN, 128), BF16),
        ),
        in_specs=[hbm] * 10,
        out_specs=(hbm, hbm, hbm),
        scratch_shapes=[
            pltpu.VMEM((NI, NJ, C), BF16),
            pltpu.VMEM((NI, NJ, C), BF16),
            pltpu.VMEM((RC * NJ, C), BF16),
            pltpu.VMEM((RC * NJ, C), BF16),
            pltpu.VMEM((RC * NJ, C), BF16),
            pltpu.VMEM((RC * NJ, C), BF16),
            pltpu.VMEM((RC * NJ, C), BF16),
            pltpu.VMEM((RC * NJ, C), BF16),
            pltpu.VMEM((BLK * NJ, C), F32),
            pltpu.VMEM((2, 6, NI, 128), F32),
            pltpu.VMEM((8 * C, 256), BF16),
            pltpu.VMEM((32, R_DEV * NI), BF16),
            pltpu.VMEM((C, PH), BF16),
            pltpu.VMEM((PH, C), BF16),
            pltpu.VMEM((HEADS, C), BF16),
            pltpu.VMEM((D, D), BF16),
            pltpu.VMEM((D, D), BF16),
            pltpu.VMEM((D, D), BF16),
            pltpu.VMEM((D, D), BF16),
            pltpu.VMEM((D, C), BF16),
            pltpu.VMEM((32, 128), BF16),
            pltpu.VMEM((C_DEV, 32, 128), BF16),
            pltpu.VMEM((D, 128), BF16),
            pltpu.VMEM((D, 128), BF16),
            pltpu.VMEM((256, D), F32),
            pltpu.VMEM((256, D), BF16),
            pltpu.VMEM((NI, D), BF16),
            pltpu.VMEM((NJ, 2 * D), F32),
            pltpu.VMEM((2, 16 * NJ, 512), BF16),
            pltpu.VMEM((2, 16 * NJ, 512), BF16),
            pltpu.VMEM((2, NI, 16 * NJ), BF16),
            pltpu.VMEM((256, D), BF16),
            pltpu.VMEM((OWNERS, OWN, WL), BF16),
            pltpu.VMEM((C_DEV, OWN, WL), BF16),
            pltpu.VMEM((C_DEV, OWN, 128), BF16),
            pltpu.VMEM((OWNERS, OWN, 128), BF16),
            pltpu.VMEM((OWN, 128), BF16),
            pltpu.VMEM((6, OWN, 128), BF16),
            dma((9,)),
            dma((STEPS,)),
            dma, dma, dma, dma, dma, dma, dma, dma, dma, dma, dma,
        ],
        compiler_params=pltpu.CompilerParams(
            collective_id=0, has_side_effects=True, vmem_limit_bytes=60 * 1024 * 1024
        ),
        name="trunk_main",
    )(pair, seq.T, w_hidden, w_back, w_bias.T, w_query, w_key, w_value, w_out, w_project)
    pair_out, seq_out = pl.pallas_call(
        pair_kernel,
        out_shape=(jax.ShapeDtypeStruct((NI, NJ, C), BF16), jax.ShapeDtypeStruct((32, NI), BF16)),
        in_specs=[hbm] * 4,
        out_specs=(hbm, hbm),
        scratch_shapes=[
            pltpu.VMEM((OWNERS, OWN, 128), BF16),
            pltpu.VMEM((6, OWN, 128), BF16),
            pltpu.VMEM((C, C), BF16),
            pltpu.VMEM((NI, 128), F32),
            pltpu.VMEM((32, NI), BF16),
            pltpu.VMEM((NI, NJ, C), BF16),
            pltpu.VMEM((NI, NJ, C), BF16),
            dma((3,)),
            dma((KSTEPS,)),
            dma,
        ],
        compiler_params=pltpu.CompilerParams(vmem_limit_bytes=60 * 1024 * 1024),
        name="pair_update",
    )(mid, left, right, w_pair)
    return pair_out, seq_out.T


def solution(mesh):
    return jax.shard_map(
        local,
        mesh=mesh,
        in_specs=(P("row", "col", None), P(None, "col")) + (P(),) * 9,
        out_specs=(P("row", "col", None), P("row", "col")),
        check_vma=False,
    )
```

```python
import functools

import jax
import jax.numpy as jnp
from jax import lax
from jax.experimental import pallas as pl
from jax.experimental.pallas import tpu as pltpu
from jax.sharding import PartitionSpec as P

HEADS = 32
EPS = 1e-05
F32 = jnp.float32
BF16 = jnp.bfloat16

R_DEV, C_DEV = 8, 32
NI, NJ, C, D, PH = 192, 48, 128, 1024, 512
OWNERS, OWN = 24, 8
RC = 16
STEPS = NI // RC
BLK = 48
SPB = BLK // RC
KSTEPS = 4
KROWS = NI // KSTEPS
SCALE = 32 ** (-0.5)
MESH = pl.DeviceIdType.MESH


def nt(a, b):
    return lax.dot_general(a, b, (((1,), (1,)), ((), ())), preferred_element_type=F32)


def tn(a, b):
    return lax.dot_general(a, b, (((0,), (0,)), ((), ())), preferred_element_type=F32)


def nn(a, b):
    return jnp.dot(a, b, preferred_element_type=F32)


def layer_norm(x, axis=-1):
    mean = jnp.mean(x, axis=axis, keepdims=True)
    cen = x - mean
    var = jnp.mean(cen * cen, axis=axis, keepdims=True)
    return cen * lax.rsqrt(var + EPS)


def row_sum(x):
    parts = [x[:, t : t + 128] for t in range(0, D, 128)]
    while len(parts) > 1:
        parts = [a + b for a, b in zip(parts[0::2], parts[1::2])]
    return jnp.sum(parts[0], axis=-1, keepdims=True)


def wide_norm(x):
    cen = x - row_sum(x) * (1.0 / D)
    return cen * lax.rsqrt(row_sum(cen * cen) * (1.0 / D) + EPS)


def iota(shape, dim):
    return lax.broadcasted_iota(jnp.int32, shape, dim)


def owner_of(col):
    y, x, z = lax.div(col, 8), lax.rem(lax.div(col, 2), 4), lax.rem(col, 2)
    xr = jnp.where(x > y, x - 1, x)
    return (y * 3 + xr) * 2 + z, x != y, y


def col_of(y, t):
    xr, z = (t // 2, t % 2) if isinstance(t, int) else (lax.div(t, 2), lax.rem(t, 2))
    x = jnp.where(xr >= y, xr + 1, xr)
    return (y * 4 + x) * 2 + z


def main_kernel(
    pair_h, seq_h, whid_h, wback_h, wbias_h, wq_h, wk_h, wv_h, wout_h, wproj_h,
    mid_h, left_o, right_o,
    pair_v, mid_v, nb0, nb1, nb2, mb0, mb1, mb2, mn_v, bias_v, bmat_v,
    seq_v, whid_v, wback_v, wbias_v, wq_v, wk_v, wv_v, wout_v, wproj_v,
    own0_v, msgs, sqk0, sqk1, raw_v, sqn, q_v, kv_v, kbd, vbd, w_v, expand_v, fac2_v, wmsg0, wmsg1, wrecv0, wrecv1, emsg, erecv, rmsg, rrecv,
    in_sem, pin_sem, mid_sem, s0_send, s0_recv, s1_send, s1_recv, w0_send, w0_recv, w1_send, w1_recv, e_send, e_recv, r_send, r_recv,
):
    me_r, me_c = lax.axis_index("row"), lax.axis_index("col")
    own_o, is_owner, me_y = owner_of(me_c)
    own_o = jnp.where(is_owner, own_o, 0)
    dest_c = 4 * me_r + me_y
    self_right = jnp.logical_and(is_owner, dest_c == me_c)

    def load(src, dst, k):
        cp = pltpu.make_async_copy(src, dst, in_sem.at[k])
        cp.start()
        return cp

    def block_y(cc):
        return lax.rem(me_y + 1 + cc, 4)

    def true_rows(k):
        if isinstance(k, int):
            return pl.ds(pl.multiple_of(block_y(k // SPB) * BLK + (k % SPB) * RC, RC), RC)
        return pl.ds(pl.multiple_of(block_y(lax.div(k, SPB)) * BLK + lax.rem(k, SPB) * RC, RC), RC)

    c_seq = load(seq_h, seq_v, 0)
    c_hid = load(whid_h, whid_v, 1)
    c_back = load(wback_h, wback_v, 2)
    c_bias = load(wbias_h, wbias_v, 3)

    def pair_copy(k):
        rows = pl.ds(pl.multiple_of(k * RC, RC), RC)
        return pltpu.make_async_copy(pair_h.at[true_rows(k)], pair_v.at[rows], pin_sem.at[k])

    for k in range(STEPS):
        pair_copy(k).start()
    c_q = load(wq_h, wq_v, 4)
    c_k = load(wk_h, wk_v, 5)
    c_v = load(wv_h, wv_v, 6)
    c_out = load(wout_h, wout_v, 7)
    c_proj = load(wproj_h, wproj_v, 8)

    barrier = pltpu.get_barrier_semaphore()
    src_r, src_y = lax.div(me_c, 4), lax.rem(me_c, 4)
    for t in range(6):
        src = col_of(src_y, t)

        @pl.when(jnp.logical_not(jnp.logical_and(src_r == me_r, src == me_c)))
        def _():
            pl.semaphore_signal(barrier, 1, device_id=(src_r, src), device_id_type=MESH)

    for s in range(1, C_DEV):
        pl.semaphore_signal(
            barrier, 1, device_id=(me_r, lax.rem(me_c + s, C_DEV)), device_id_type=MESH
        )

    c_seq.wait()
    lane32 = iota((32, 128), 1)
    base = pl.multiple_of((me_r * 3 // 2) * 128, 128)
    own = seq_v[:, pl.ds(base, 256)].astype(F32)
    own = jnp.where(me_r % 2 == 1, pltpu.roll(own, 192, 1), own)
    own0_v[...] = own[:, 0:128].astype(BF16)
    own1 = own[:, 128:256]
    for c in range(C_DEV):
        t, o = (c * NJ) // 128, (c * NJ) % 128
        keys = seq_v[:, t * 128 : t * 128 + 128].astype(F32)
        if o + NJ > 128:
            keys = jnp.where(lane32 >= o, keys, seq_v[:, t * 128 + 128 : t * 128 + 256].astype(F32))
        if o != 64:
            keys = pltpu.roll(keys, (64 - o) % 128, 1)
        msgs[c] = jnp.where(lane32 < 64, own1, jnp.where(lane32 < 112, keys, 0.0)).astype(BF16)

    pl.semaphore_wait(
        barrier, C_DEV - 1 + jnp.where(is_owner, R_DEV, 0) - jnp.where(self_right, 1, 0)
    )
    my_slab = pl.ds(pl.multiple_of(me_c * 32, 32), 32)
    for s in range(1, C_DEV):
        dst = lax.rem(me_c + s, C_DEV)
        pltpu.make_async_remote_copy(
            msgs.at[dst], sqk1.at[my_slab], s1_send, s1_recv, device_id=(me_r, dst), device_id_type=MESH
        ).start()
    for s in range(1, C_DEV):
        dst = lax.rem(me_c + s, C_DEV)
        pltpu.make_async_remote_copy(
            own0_v, sqk0.at[my_slab], s0_send, s0_recv, device_id=(me_r, dst), device_id_type=MESH
        ).start()
    pltpu.make_async_copy(msgs.at[me_c], sqk1.at[my_slab], s1_recv).start()
    pltpu.make_async_copy(own0_v, sqk0.at[my_slab], s0_recv).start()

    c_bias.wait()
    spread = jnp.where(
        iota((32, 256), 0) == (iota((32, 256), 1) // 128) * 16 + iota((32, 256), 1) % 16, 1.0, 0.0
    ).astype(BF16)
    wide = tn(wbias_v[...], spread)
    slot = (iota((C, 256), 1) % 128) // 16
    for j8 in range(8):
        bmat_v[j8 * C : (j8 + 1) * C, :] = jnp.where(slot == j8, wide, 0.0).astype(BF16)
    head_lane = iota((128, D), 0) == iota((128, D), 1) // 32
    expand_v[0:128] = jnp.where(head_lane, 1.0, 0.0).astype(BF16)
    expand_v[128:256] = jnp.where(head_lane, 1.0, 0.0).astype(BF16)

    nb, mb = (nb0, nb1, nb2), (mb0, mb1, mb2)

    def rows_of(k):
        return pl.ds(pl.multiple_of(k * RC, RC), RC)

    def stage_norm(k, s):
        x = pair_v[rows_of(k)].astype(F32).reshape(RC * NJ, C)
        nb[s][...] = layer_norm(x).astype(BF16)

    def stage_hidden(k, s):
        hid = jnp.maximum(nn(nb[s][...], whid_v[...]), 0.0).astype(BF16)
        x = pair_v[rows_of(k)].astype(F32).reshape(RC * NJ, C)
        mid = (x + nn(hid, wback_v[...])).astype(BF16)
        mid_v[rows_of(k)] = mid.reshape(RC, NJ, C)
        mb[s][...] = mid

    def stage_mid(s):
        mn_v[s * RC * NJ : (s + 1) * RC * NJ] = layer_norm(mb[s][...].astype(F32))

    def stage_bias(b):
        blocks = []
        for jb in range(6):
            cols = []
            for j8 in range(8):
                j = jb * 8 + j8
                cols.append(
                    jnp.concatenate(
                        [mn_v[pl.ds(h * 8 * NJ + j, 8, stride=NJ), :] for h in range(BLK // 8)], axis=0
                    ).astype(BF16)
                )
            blocks.append(jnp.concatenate(cols, axis=1))
        out = nn(jnp.concatenate(blocks, axis=0), bmat_v[...])
        for jb in range(6):
            for g in range(2):
                bias_v[g, jb, pl.ds(pl.multiple_of(b * BLK, BLK), BLK), :] = out[
                    jb * BLK : (jb + 1) * BLK, g * 128 : (g + 1) * 128
                ]

    def mid_out(k):
        return pltpu.make_async_copy(mid_v.at[rows_of(k)], mid_h.at[true_rows(k)], mid_sem)

    def pair_block(t, _, first=False):
        for u in range(3):
            pair_copy(3 * t + 2 + u).wait()
        if first:
            stage_norm(0, 0)
            stage_hidden(0, 0)
            stage_norm(1, 1)
        else:
            stage_bias(t - 1)
        for u in range(3):
            k, s = 3 * t + 1 + u, (1 + u) % 3
            stage_hidden(k, s)
            stage_norm(k + 1, (s + 1) % 3)
            stage_mid(u)
        for u in range(3):
            mid_out(3 * t + u).start()
        return 0

    c_hid.wait()
    c_back.wait()
    pair_copy(0).wait()
    pair_copy(1).wait()
    pair_block(0, 0, first=True)
    lax.fori_loop(1, 3, pair_block, 0)
    stage_bias(2)

    ident = jnp.where(iota((128, 128), 0) == iota((128, 128), 1), 1.0, 0.0).astype(BF16)

    def norm_rows(k, _):
        for u in range(4):
            rows = pl.ds(pl.multiple_of(k * 64 + u * 16, 16), 16)
            sqn[rows, :] = wide_norm(raw_v[rows, :]).astype(BF16)
        return 0

    pltpu.make_async_copy(sqk1, sqk1, s1_recv).wait()
    raw_v[128:256] = nt(ident, sqk1[...])
    lax.fori_loop(2, 4, norm_rows, 0)
    c_k.wait()
    c_v.wait()
    kv_v[:, 0:D] = nn(sqn[NI : NI + NJ], wk_v[...])
    kv_v[:, D : 2 * D] = nn(sqn[NI : NI + NJ], wv_v[...])
    head_here = iota((16, 512), 0) == iota((16, 512), 1) // 32

    def spread_keys(j4, _):
        for u in range(4):
            j = j4 * 4 + u
            dst = pl.ds(pl.multiple_of(j * 16, 16), 16)
            for g in range(2):
                krow = jnp.broadcast_to(kv_v[pl.ds(j, 1), g * 512 : (g + 1) * 512], (16, 512))
                vrow = jnp.broadcast_to(kv_v[pl.ds(j, 1), D + g * 512 : D + (g + 1) * 512], (16, 512))
                kbd[g, dst, :] = jnp.where(head_here, krow, 0.0).astype(BF16)
                vbd[g, dst, :] = jnp.where(head_here, vrow, 0.0).astype(BF16)
        return 0

    lax.fori_loop(0, NJ // 4, spread_keys, 0)
    pltpu.make_async_copy(sqk0, sqk0, s0_recv).wait()
    raw_v[0:128] = nt(ident, sqk0[...])
    lax.fori_loop(0, 2, norm_rows, 0)
    c_q.wait()
    q_v[...] = nn(sqn[:NI], wq_v[...]).astype(BF16)

    def attend(first, count):
        n = count * BLK
        lane = iota((n, 128), 1)
        q = [
            q_v[pl.ds(pl.multiple_of(block_y(cc) * BLK, 16), BLK), :] for cc in range(first, first + count)
        ]
        q = q[0] if count == 1 else jnp.concatenate(q, axis=0)
        here = slice(first * BLK, first * BLK + n)
        parts = []
        for g in range(2):
            scores = nt(q[:, g * 512 : (g + 1) * 512], kbd[g])
            tiles = [scores[:, jb * 128 : (jb + 1) * 128] * SCALE + bias_v[g, jb, here, :] for jb in range(6)]
            top = functools.reduce(jnp.maximum, tiles)
            for shift in (16, 32, 64):
                top = jnp.maximum(top, pltpu.roll(top, shift, 1))
            total = None
            for jb in range(6):
                w = jnp.exp(tiles[jb] - top)
                w_v[g, here, jb * 128 : (jb + 1) * 128] = w.astype(BF16)
                total = w if total is None else total + w
            for shift in (16, 32, 64):
                total = total + pltpu.roll(total, shift, 1)
            high = top.astype(BF16).astype(F32)
            middle = (top - high).astype(BF16).astype(F32)
            low = (top - high) - middle
            parts.append((high, middle, low, total))
        stats = jnp.zeros((n, 128), F32)
        for p in range(4):
            for g in range(2):
                stats = jnp.where(lane // 16 == p * 2 + g, parts[g][p], stats)
        slots = slice(first * 6, (first + count) * 6)
        for g in range(2):
            msg, land, ssem, rsem = (
                (wmsg0, wrecv0, w0_send, w0_recv), (wmsg1, wrecv1, w1_send, w1_recv)
            )[g]
            weighted = nn(w_v[g, here, :], vbd[g])
            msg[slots, :, 0:512] = weighted.reshape(count * 6, OWN, 512).astype(BF16)
            if g == 0:
                msg[slots, :, 512:640] = stats.reshape(count * 6, OWN, 128).astype(BF16)
            for i in range(count * 6 if first < 3 else 0):
                cc, t = first + i // 6, i % 6
                dst = col_of(block_y(cc), t)

                def start():
                    pltpu.make_async_remote_copy(
                        msg.at[cc * 6 + t], land.at[me_c], ssem, rsem,
                        device_id=(me_r, dst), device_id_type=MESH,
                    ).start()

                start()
    attend(0, 3)
    pair_copy(11).wait()
    stage_hidden(10, 1)
    stage_norm(11, 2)
    stage_mid(0)
    stage_hidden(11, 2)
    stage_mid(1)
    stage_mid(2)
    stage_bias(3)
    for k in range(9, 12):
        mid_out(k).start()
    attend(3, 1)
    for t in range(6):
        dst = col_of(block_y(3), t)
        halves = ((wmsg0, wrecv0, w0_send, w0_recv), (wmsg1, wrecv1, w1_send, w1_recv))

        @pl.when(dst != me_c)
        def _():
            for msg, land, ssem, rsem in halves:
                pltpu.make_async_remote_copy(
                    msg.at[18 + t], land.at[me_c], ssem, rsem, device_id=(me_r, dst), device_id_type=MESH
                ).start()

        @pl.when(dst == me_c)
        def _():
            for msg, land, _ssem, rsem in halves:
                pltpu.make_async_copy(msg.at[18 + t], land.at[me_c], rsem).start()


    @pl.when(is_owner)
    def _():
        resid = raw_v[pl.ds(pl.multiple_of(own_o * 8, 8), 8), :]
        c_out.wait()
        c_proj.wait()
        pltpu.make_async_copy(wrecv0, wrecv0, w0_recv).wait()
        st = wrecv0[:, :, 512:640].astype(F32).reshape(C_DEV * OWN, 128)
        m = (st + pltpu.roll(st, 96, 1)) + pltpu.roll(st, 64, 1)
        den = pltpu.roll(st, 32, 1)
        m3 = m.reshape(C_DEV, OWN, 128)
        top = jnp.max(m3, axis=0)
        fac = jnp.where(iota((C_DEV, OWN, 128), 2) < 32, jnp.exp(jnp.minimum(m3 - top[None], 0.0)), 0.0)
        whole = jnp.sum(fac * den.reshape(C_DEV, OWN, 128), axis=0)
        whole = jnp.where(iota((OWN, 128), 1) < 32, whole, 1.0)
        fac = (fac / whole[None]).reshape(C_DEV * OWN, 128)
        high = fac.astype(BF16)
        low = (fac - high.astype(F32)).astype(BF16)
        fac2_v[...] = jnp.concatenate([high, low], axis=1)
        update = resid
        for g in range(2):
            land = (wrecv0, wrecv1)[g]
            half = slice(g * 512, (g + 1) * 512)
            if g == 1:
                pltpu.make_async_copy(wrecv1, wrecv1, w1_recv).wait()
            wide = nn(fac2_v[...], expand_v[:, half]).reshape(C_DEV, OWN, 512)
            attended = jnp.sum(wide * land[:, :, 0:512].astype(F32), axis=0).astype(BF16)
            update = update + nn(attended, wout_v[half, :])
        seq_new = update.astype(BF16).astype(F32)
        proj = nn(wide_norm(seq_new).astype(BF16), wproj_v[...]).astype(BF16).astype(F32)
        turned = pltpu.roll(proj, 64, 1)
        lane8 = iota((OWN, 128), 1)
        right = jnp.where(lane8 < 64, turned, proj).astype(BF16)
        rmsg[...] = right
        for c in range(C_DEV):
            tile = seq_new[:, (c // 4) * 128 : (c // 4) * 128 + 128]
            if c % 4 != 2:
                tile = pltpu.roll(tile, (192 - 32 * (c % 4)) % 128, 1)
            emsg[c] = jnp.where(lane8 < 64, proj, tile).astype(BF16)

        slot = lax.rem(own_o, 6)
        for r in range(R_DEV):
            here = jnp.logical_and(r == me_r, dest_c == me_c)

            @pl.when(jnp.logical_not(here))
            def _():
                pltpu.make_async_remote_copy(
                    rmsg, rrecv.at[slot], r_send, r_recv, device_id=(r, dest_c), device_id_type=MESH
                ).start()

            @pl.when(here)
            def _():
                pltpu.make_async_copy(rmsg, rrecv.at[slot], r_recv).start()

        for s in range(1, C_DEV):
            dst = lax.rem(me_c + (s + 15) % 31 + 1, C_DEV)
            pltpu.make_async_remote_copy(
                emsg.at[dst], erecv.at[own_o], e_send, e_recv, device_id=(me_r, dst), device_id_type=MESH
            ).start()
        pltpu.make_async_copy(emsg.at[me_c], erecv.at[own_o], e_recv).start()

    @pl.when(jnp.logical_not(is_owner))
    def _():
        c_out.wait()
        c_proj.wait()

    pltpu.make_async_copy(mid_v, mid_h, mid_sem).wait()
    pltpu.make_async_copy(msgs.at[0 : C_DEV - 1], msgs.at[0 : C_DEV - 1], s1_send).wait()
    others = pl.ds(0, 32 * (C_DEV - 1))
    pltpu.make_async_copy(sqk0.at[others], sqk0.at[others], s0_send).wait()

    def sent_rows(i, _):
        @pl.when(col_of(block_y(lax.div(i, 6)), lax.rem(i, 6)) != me_c)
        def _():
            pltpu.make_async_copy(wmsg0.at[i], wmsg0.at[i], w0_send).wait()
            pltpu.make_async_copy(wmsg1.at[i], wmsg1.at[i], w1_send).wait()

        return 0

    lax.fori_loop(0, OWNERS, sent_rows, 0)

    pltpu.make_async_copy(rrecv, rrecv, r_recv).wait()
    right_put = pltpu.make_async_copy(rrecv, right_o, in_sem.at[0])
    right_put.start()
    pltpu.make_async_copy(erecv, erecv, e_recv).wait()
    left_put = pltpu.make_async_copy(erecv, left_o, in_sem.at[1])
    left_put.start()

    @pl.when(is_owner)
    def _():
        pltpu.make_async_copy(emsg.at[0 : C_DEV - 1], emsg.at[0 : C_DEV - 1], e_send).wait()

        def sent_right(r, _):
            @pl.when(jnp.logical_not(jnp.logical_and(r == me_r, dest_c == me_c)))
            def _():
                pltpu.make_async_copy(rmsg, rmsg, r_send).wait()

            return 0

        lax.fori_loop(0, R_DEV, sent_right, 0)
    right_put.wait()
    left_put.wait()


def pair_kernel(
    mid_h, left_h, right_h, wpair_h, out_h, seq_h,
    left_b, right_b, wpair_v, left_v, seq_v, mid_v, out_v, small_sem, in_sem, out_sem,
):
    spans = [pl.ds(k * KROWS, KROWS) for k in range(KSTEPS)]
    small = [
        pltpu.make_async_copy(src, dst, small_sem.at[k])
        for k, (src, dst) in enumerate(((left_h, left_b), (right_h, right_b), (wpair_h, wpair_v)))
    ]
    for cp in small:
        cp.start()
    fetches = [pltpu.make_async_copy(mid_h.at[r], mid_v.at[r], in_sem.at[k]) for k, r in enumerate(spans)]
    for cp in fetches:
        cp.start()
    for cp in small:
        cp.wait()
    lane = iota((NJ, C), 1)
    right = right_b[...].astype(F32).reshape(NJ, C)
    scale = jnp.where(lane < 64, right, 1.0)
    shift = jnp.where(lane < 64, 0.0, -right)
    arrived = left_b[...].astype(F32).reshape(NI, C)
    left_v[...] = jnp.where(iota((NI, C), 1) < 64, arrived, pltpu.roll(arrived, 64, 1))
    pick = jnp.where(iota((32, C), 1) == iota((32, C), 0) + 64, 1.0, 0.0).astype(BF16)
    seq_v[...] = nt(pick, left_b[...].reshape(NI, C)).astype(BF16)
    seq_put = pltpu.make_async_copy(seq_v, seq_h, small_sem.at[0])
    seq_put.start()

    def step(k, _):
        rows = pl.ds(pl.multiple_of(k * KROWS, KROWS), KROWS)
        pltpu.make_async_copy(mid_h.at[rows], mid_v.at[rows], in_sem.at[k]).wait()
        left = left_v[rows, :].reshape(KROWS, 1, C)
        feature = (left * scale[None] + shift[None]).astype(BF16).reshape(KROWS * NJ, C)
        update = nn(feature, wpair_v[...])
        mid = mid_v[rows].astype(F32).reshape(KROWS * NJ, C)
        out_v[rows] = (mid + update).astype(BF16).reshape(KROWS, NJ, C)
        pltpu.make_async_copy(out_v.at[rows], out_h.at[rows], out_sem).start()
        return 0

    lax.fori_loop(0, KSTEPS, step, 0)
    seq_put.wait()
    pltpu.make_async_copy(out_v, out_h, out_sem).wait()


def local(pair, seq, w_hidden, w_back, w_bias, w_query, w_key, w_value, w_out, w_project, w_pair):
    hbm = pl.BlockSpec(memory_space=pl.ANY)
    dma = pltpu.SemaphoreType.DMA
    mid, left, right = pl.pallas_call(
        main_kernel,
        out_shape=(
            jax.ShapeDtypeStruct((NI, NJ, C), BF16),
            jax.ShapeDtypeStruct((OWNERS, OWN, 128), BF16),
            jax.ShapeDtypeStruct((6, OWN, 128), BF16),
        ),
        in_specs=[hbm] * 10,
        out_specs=(hbm, hbm, hbm),
        scratch_shapes=[
            pltpu.VMEM((NI, NJ, C), BF16),
            pltpu.VMEM((NI, NJ, C), BF16),
            pltpu.VMEM((RC * NJ, C), BF16),
            pltpu.VMEM((RC * NJ, C), BF16),
            pltpu.VMEM((RC * NJ, C), BF16),
            pltpu.VMEM((RC * NJ, C), BF16),
            pltpu.VMEM((RC * NJ, C), BF16),
            pltpu.VMEM((RC * NJ, C), BF16),
            pltpu.VMEM((BLK * NJ, C), F32),
            pltpu.VMEM((2, 6, NI, 128), F32),
            pltpu.VMEM((8 * C, 256), BF16),
            pltpu.VMEM((32, R_DEV * NI), BF16),
            pltpu.VMEM((C, PH), BF16),
            pltpu.VMEM((PH, C), BF16),
            pltpu.VMEM((HEADS, C), BF16),
            pltpu.VMEM((D, D), BF16),
            pltpu.VMEM((D, D), BF16),
            pltpu.VMEM((D, D), BF16),
            pltpu.VMEM((D, D), BF16),
            pltpu.VMEM((D, C), BF16),
            pltpu.VMEM((32, 128), BF16),
            pltpu.VMEM((C_DEV, 32, 128), BF16),
            pltpu.VMEM((D, 128), BF16),
            pltpu.VMEM((D, 128), BF16),
            pltpu.VMEM((256, D), F32),
            pltpu.VMEM((256, D), BF16),
            pltpu.VMEM((NI, D), BF16),
            pltpu.VMEM((NJ, 2 * D), F32),
            pltpu.VMEM((2, 16 * NJ, 512), BF16),
            pltpu.VMEM((2, 16 * NJ, 512), BF16),
            pltpu.VMEM((2, NI, 16 * NJ), BF16),
            pltpu.VMEM((256, D), BF16),
            pltpu.VMEM((C_DEV * OWN, 256), BF16),
            pltpu.VMEM((OWNERS, OWN, 640), BF16),
            pltpu.VMEM((OWNERS, OWN, 512), BF16),
            pltpu.VMEM((C_DEV, OWN, 640), BF16),
            pltpu.VMEM((C_DEV, OWN, 512), BF16),
            pltpu.VMEM((C_DEV, OWN, 128), BF16),
            pltpu.VMEM((OWNERS, OWN, 128), BF16),
            pltpu.VMEM((OWN, 128), BF16),
            pltpu.VMEM((6, OWN, 128), BF16),
            dma((9,)),
            dma((STEPS,)),
            dma, dma, dma, dma, dma, dma, dma, dma, dma, dma, dma, dma, dma,
        ],
        compiler_params=pltpu.CompilerParams(
            collective_id=0, has_side_effects=True, vmem_limit_bytes=60 * 1024 * 1024
        ),
        name="trunk_main",
    )(pair, seq.T, w_hidden, w_back, w_bias.T, w_query, w_key, w_value, w_out, w_project)
    pair_out, seq_out = pl.pallas_call(
        pair_kernel,
        out_shape=(jax.ShapeDtypeStruct((NI, NJ, C), BF16), jax.ShapeDtypeStruct((32, NI), BF16)),
        in_specs=[hbm] * 4,
        out_specs=(hbm, hbm),
        scratch_shapes=[
            pltpu.VMEM((OWNERS, OWN, 128), BF16),
            pltpu.VMEM((6, OWN, 128), BF16),
            pltpu.VMEM((C, C), BF16),
            pltpu.VMEM((NI, 128), F32),
            pltpu.VMEM((32, NI), BF16),
            pltpu.VMEM((NI, NJ, C), BF16),
            pltpu.VMEM((NI, NJ, C), BF16),
            dma((3,)),
            dma((KSTEPS,)),
            dma,
        ],
        compiler_params=pltpu.CompilerParams(vmem_limit_bytes=60 * 1024 * 1024),
        name="pair_update",
    )(mid, left, right, w_pair)
    return pair_out, seq_out.T


def solution(mesh):
    return jax.shard_map(
        local,
        mesh=mesh,
        in_specs=(P("row", "col", None), P(None, "col")) + (P(),) * 9,
        out_specs=(P("row", "col", None), P("row", "col")),
        check_vma=False,
    )
```

```python
import functools

import jax
import jax.numpy as jnp
from jax import lax
from jax.experimental import pallas as pl
from jax.experimental.pallas import tpu as pltpu
from jax.sharding import PartitionSpec as P

HEADS = 32
EPS = 1e-05
F32 = jnp.float32
BF16 = jnp.bfloat16

R_DEV, C_DEV = 8, 32
NI, NJ, C, D, PH = 192, 48, 128, 1024, 512
OWNERS, OWN = 24, 8
RC = 16
STEPS = NI // RC
BLK = 48
SPB = BLK // RC
KSTEPS = 4
KROWS = NI // KSTEPS
SCALE = 32 ** (-0.5)
MESH = pl.DeviceIdType.MESH


def nt(a, b):
    return lax.dot_general(a, b, (((1,), (1,)), ((), ())), preferred_element_type=F32)


def tn(a, b):
    return lax.dot_general(a, b, (((0,), (0,)), ((), ())), preferred_element_type=F32)


def nn(a, b):
    return jnp.dot(a, b, preferred_element_type=F32)


def layer_norm(x, axis=-1):
    mean = jnp.mean(x, axis=axis, keepdims=True)
    cen = x - mean
    var = jnp.mean(cen * cen, axis=axis, keepdims=True)
    return cen * lax.rsqrt(var + EPS)


def row_sum(x):
    parts = [x[:, t : t + 128] for t in range(0, D, 128)]
    while len(parts) > 1:
        parts = [a + b for a, b in zip(parts[0::2], parts[1::2])]
    return jnp.sum(parts[0], axis=-1, keepdims=True)


def wide_norm(x):
    cen = x - row_sum(x) * (1.0 / D)
    return cen * lax.rsqrt(row_sum(cen * cen) * (1.0 / D) + EPS)


def iota(shape, dim):
    return lax.broadcasted_iota(jnp.int32, shape, dim)


def owner_of(col):
    y, x, z = lax.div(col, 8), lax.rem(lax.div(col, 2), 4), lax.rem(col, 2)
    xr = jnp.where(x > y, x - 1, x)
    return (y * 3 + xr) * 2 + z, x != y, y


def col_of(y, t):
    xr, z = (t // 2, t % 2) if isinstance(t, int) else (lax.div(t, 2), lax.rem(t, 2))
    x = jnp.where(xr >= y, xr + 1, xr)
    return (y * 4 + x) * 2 + z


def main_kernel(
    pair_h, seq_h, whid_h, wback_h, wbias_h, wq_h, wk_h, wv_h, wout_h, wproj_h,
    mid_h, left_o, right_o,
    pair_v, mid_v, nb0, nb1, nb2, mb0, mb1, mb2, mn_v, bias_v, bmat_v,
    seq_v, whid_v, wback_v, wbias_v, wq_v, wk_v, wv_v, wout_v, wproj_v,
    own0_v, msgs, sqk0, sqk1, raw_v, sqn, q_v, kv_v, kbd, vbd, w_v, expand_v, fac2_v, wmsg0, wmsg1, wrecv0, wrecv1, emsg, erecv, rmsg, rrecv,
    in_sem, pin_sem, mid_sem, s0_send, s0_recv, s1_send, s1_recv, w0_send, w0_recv, w1_send, w1_recv, e_send, e_recv, r_send, r_recv,
):
    me_r, me_c = lax.axis_index("row"), lax.axis_index("col")
    own_o, is_owner, me_y = owner_of(me_c)
    own_o = jnp.where(is_owner, own_o, 0)
    dest_c = 4 * me_r + me_y
    self_right = jnp.logical_and(is_owner, dest_c == me_c)

    def load(src, dst, k):
        cp = pltpu.make_async_copy(src, dst, in_sem.at[k])
        cp.start()
        return cp

    def block_y(cc):
        return lax.rem(me_y + 1 + cc, 4)

    def true_rows(k):
        if isinstance(k, int):
            return pl.ds(pl.multiple_of(block_y(k // SPB) * BLK + (k % SPB) * RC, RC), RC)
        return pl.ds(pl.multiple_of(block_y(lax.div(k, SPB)) * BLK + lax.rem(k, SPB) * RC, RC), RC)

    c_seq = load(seq_h, seq_v, 0)
    c_hid = load(whid_h, whid_v, 1)
    c_back = load(wback_h, wback_v, 2)
    c_bias = load(wbias_h, wbias_v, 3)

    def pair_copy(k):
        rows = pl.ds(pl.multiple_of(k * RC, RC), RC)
        return pltpu.make_async_copy(pair_h.at[true_rows(k)], pair_v.at[rows], pin_sem.at[k])

    for k in range(STEPS):
        pair_copy(k).start()
    c_q = load(wq_h, wq_v, 4)
    c_k = load(wk_h, wk_v, 5)
    c_v = load(wv_h, wv_v, 6)
    c_out = load(wout_h, wout_v, 7)
    c_proj = load(wproj_h, wproj_v, 8)

    barrier = pltpu.get_barrier_semaphore()
    src_r, src_y = lax.div(me_c, 4), lax.rem(me_c, 4)
    for t in range(6):
        src = col_of(src_y, t)

        @pl.when(jnp.logical_not(jnp.logical_and(src_r == me_r, src == me_c)))
        def _():
            pl.semaphore_signal(barrier, 1, device_id=(src_r, src), device_id_type=MESH)

    for s in range(1, C_DEV):
        pl.semaphore_signal(
            barrier, 1, device_id=(me_r, lax.rem(me_c + s, C_DEV)), device_id_type=MESH
        )

    c_seq.wait()
    lane32 = iota((32, 128), 1)
    base = pl.multiple_of((me_r * 3 // 2) * 128, 128)
    own = seq_v[:, pl.ds(base, 256)].astype(F32)
    own = jnp.where(me_r % 2 == 1, pltpu.roll(own, 192, 1), own)
    own0_v[...] = own[:, 0:128].astype(BF16)
    own1 = own[:, 128:256]
    for c in range(C_DEV):
        t, o = (c * NJ) // 128, (c * NJ) % 128
        keys = seq_v[:, t * 128 : t * 128 + 128].astype(F32)
        if o + NJ > 128:
            keys = jnp.where(lane32 >= o, keys, seq_v[:, t * 128 + 128 : t * 128 + 256].astype(F32))
        if o != 64:
            keys = pltpu.roll(keys, (64 - o) % 128, 1)
        msgs[c] = jnp.where(lane32 < 64, own1, jnp.where(lane32 < 112, keys, 0.0)).astype(BF16)

    pl.semaphore_wait(
        barrier, C_DEV - 1 + jnp.where(is_owner, R_DEV, 0) - jnp.where(self_right, 1, 0)
    )
    my_slab = pl.ds(pl.multiple_of(me_c * 32, 32), 32)
    for s in range(1, C_DEV):
        dst = lax.rem(me_c + s, C_DEV)
        pltpu.make_async_remote_copy(
            msgs.at[dst], sqk1.at[my_slab], s1_send, s1_recv, device_id=(me_r, dst), device_id_type=MESH
        ).start()
    for s in range(1, C_DEV):
        dst = lax.rem(me_c + s, C_DEV)
        pltpu.make_async_remote_copy(
            own0_v, sqk0.at[my_slab], s0_send, s0_recv, device_id=(me_r, dst), device_id_type=MESH
        ).start()
    pltpu.make_async_copy(msgs.at[me_c], sqk1.at[my_slab], s1_recv).start()
    pltpu.make_async_copy(own0_v, sqk0.at[my_slab], s0_recv).start()

    c_bias.wait()
    spread = jnp.where(
        iota((32, 256), 0) == (iota((32, 256), 1) // 128) * 16 + iota((32, 256), 1) % 16, 1.0, 0.0
    ).astype(BF16)
    wide = tn(wbias_v[...], spread)
    slot = (iota((C, 256), 1) % 128) // 16
    for j8 in range(8):
        bmat_v[j8 * C : (j8 + 1) * C, :] = jnp.where(slot == j8, wide, 0.0).astype(BF16)
    head_lane = iota((128, D), 0) == iota((128, D), 1) // 32
    expand_v[0:128] = jnp.where(head_lane, 1.0, 0.0).astype(BF16)
    expand_v[128:256] = jnp.where(head_lane, 1.0, 0.0).astype(BF16)

    nb, mb = (nb0, nb1, nb2), (mb0, mb1, mb2)

    def rows_of(k):
        return pl.ds(pl.multiple_of(k * RC, RC), RC)

    def stage_norm(k, s):
        x = pair_v[rows_of(k)].astype(F32).reshape(RC * NJ, C)
        nb[s][...] = layer_norm(x).astype(BF16)

    def stage_hidden(k, s):
        hid = jnp.maximum(nn(nb[s][...], whid_v[...]), 0.0).astype(BF16)
        x = pair_v[rows_of(k)].astype(F32).reshape(RC * NJ, C)
        mid = (x + nn(hid, wback_v[...])).astype(BF16)
        mid_v[rows_of(k)] = mid.reshape(RC, NJ, C)
        mb[s][...] = mid

    def stage_mid(s):
        mn_v[s * RC * NJ : (s + 1) * RC * NJ] = layer_norm(mb[s][...].astype(F32))

    def stage_bias(b):
        blocks = []
        for jb in range(6):
            cols = []
            for j8 in range(8):
                j = jb * 8 + j8
                cols.append(
                    jnp.concatenate(
                        [mn_v[pl.ds(h * 8 * NJ + j, 8, stride=NJ), :] for h in range(BLK // 8)], axis=0
                    ).astype(BF16)
                )
            blocks.append(jnp.concatenate(cols, axis=1))
        out = nn(jnp.concatenate(blocks, axis=0), bmat_v[...])
        for jb in range(6):
            for g in range(2):
                bias_v[g, jb, pl.ds(pl.multiple_of(b * BLK, BLK), BLK), :] = out[
                    jb * BLK : (jb + 1) * BLK, g * 128 : (g + 1) * 128
                ]

    def mid_out(k):
        return pltpu.make_async_copy(mid_v.at[rows_of(k)], mid_h.at[true_rows(k)], mid_sem)

    def pair_block(t, _, first=False):
        for u in range(3):
            pair_copy(3 * t + 2 + u).wait()
        if first:
            stage_norm(0, 0)
            stage_hidden(0, 0)
            stage_norm(1, 1)
        else:
            stage_bias(t - 1)
        for u in range(3):
            k, s = 3 * t + 1 + u, (1 + u) % 3
            stage_hidden(k, s)
            stage_norm(k + 1, (s + 1) % 3)
            stage_mid(u)
        for u in range(3):
            mid_out(3 * t + u).start()
        return 0

    c_hid.wait()
    c_back.wait()
    pair_copy(0).wait()
    pair_copy(1).wait()
    pair_block(0, 0, first=True)
    lax.fori_loop(1, 3, pair_block, 0)
    stage_bias(2)

    ident = jnp.where(iota((128, 128), 0) == iota((128, 128), 1), 1.0, 0.0).astype(BF16)

    def norm_rows(k, _):
        for u in range(4):
            rows = pl.ds(pl.multiple_of(k * 64 + u * 16, 16), 16)
            sqn[rows, :] = wide_norm(raw_v[rows, :]).astype(BF16)
        return 0

    pltpu.make_async_copy(sqk1, sqk1, s1_recv).wait()
    raw_v[128:256] = nt(ident, sqk1[...])
    lax.fori_loop(2, 4, norm_rows, 0)
    c_k.wait()
    c_v.wait()
    kv_v[:, 0:D] = nn(sqn[NI : NI + NJ], wk_v[...])
    kv_v[:, D : 2 * D] = nn(sqn[NI : NI + NJ], wv_v[...])
    head_here = iota((16, 512), 0) == iota((16, 512), 1) // 32

    def spread_keys(j4, _):
        for u in range(4):
            j = j4 * 4 + u
            dst = pl.ds(pl.multiple_of(j * 16, 16), 16)
            for g in range(2):
                krow = jnp.broadcast_to(kv_v[pl.ds(j, 1), g * 512 : (g + 1) * 512], (16, 512))
                vrow = jnp.broadcast_to(kv_v[pl.ds(j, 1), D + g * 512 : D + (g + 1) * 512], (16, 512))
                kbd[g, dst, :] = jnp.where(head_here, krow, 0.0).astype(BF16)
                vbd[g, dst, :] = jnp.where(head_here, vrow, 0.0).astype(BF16)
        return 0

    lax.fori_loop(0, NJ // 4, spread_keys, 0)
    pltpu.make_async_copy(sqk0, sqk0, s0_recv).wait()
    raw_v[0:128] = nt(ident, sqk0[...])
    lax.fori_loop(0, 2, norm_rows, 0)
    c_q.wait()
    q_v[...] = nn(sqn[:NI], wq_v[...]).astype(BF16)

    def attend(first, count):
        n = count * BLK
        lane = iota((n, 128), 1)
        q = [
            q_v[pl.ds(pl.multiple_of(block_y(cc) * BLK, 16), BLK), :] for cc in range(first, first + count)
        ]
        q = q[0] if count == 1 else jnp.concatenate(q, axis=0)
        here = slice(first * BLK, first * BLK + n)
        parts = []
        for g in range(2):
            scores = nt(q[:, g * 512 : (g + 1) * 512], kbd[g])
            tiles = [scores[:, jb * 128 : (jb + 1) * 128] * SCALE + bias_v[g, jb, here, :] for jb in range(6)]
            top = functools.reduce(jnp.maximum, tiles)
            for shift in (16, 32, 64):
                top = jnp.maximum(top, pltpu.roll(top, shift, 1))
            total = None
            for jb in range(6):
                w = jnp.exp(tiles[jb] - top)
                w_v[g, here, jb * 128 : (jb + 1) * 128] = w.astype(BF16)
                total = w if total is None else total + w
            for shift in (16, 32, 64):
                total = total + pltpu.roll(total, shift, 1)
            high = top.astype(BF16).astype(F32)
            middle = (top - high).astype(BF16).astype(F32)
            low = (top - high) - middle
            parts.append((high, middle, low, total))
        stats = jnp.zeros((n, 128), F32)
        for p in range(4):
            for g in range(2):
                stats = jnp.where(lane // 16 == p * 2 + g, parts[g][p], stats)
        slots = slice(first * 6, (first + count) * 6)
        for g in range(2):
            msg, land, ssem, rsem = (
                (wmsg0, wrecv0, w0_send, w0_recv), (wmsg1, wrecv1, w1_send, w1_recv)
            )[g]
            weighted = nn(w_v[g, here, :], vbd[g])
            msg[slots, :, 0:512] = weighted.reshape(count * 6, OWN, 512).astype(BF16)
            if g == 0:
                msg[slots, :, 512:640] = stats.reshape(count * 6, OWN, 128).astype(BF16)
            for i in range(count * 6 if first < 3 else 0):
                cc, t = first + i // 6, i % 6
                dst = col_of(block_y(cc), t)

                def start():
                    pltpu.make_async_remote_copy(
                        msg.at[cc * 6 + t], land.at[me_c], ssem, rsem,
                        device_id=(me_r, dst), device_id_type=MESH,
                    ).start()

                start()
    attend(0, 3)
    pair_copy(11).wait()
    stage_hidden(10, 1)
    stage_norm(11, 2)
    stage_mid(0)
    stage_hidden(11, 2)
    stage_mid(1)
    stage_mid(2)
    stage_bias(3)
    for k in range(9, 12):
        mid_out(k).start()
    attend(3, 1)
    for t in range(6):
        dst = col_of(block_y(3), t)
        halves = ((wmsg0, wrecv0, w0_send, w0_recv), (wmsg1, wrecv1, w1_send, w1_recv))

        @pl.when(dst != me_c)
        def _():
            for msg, land, ssem, rsem in halves:
                pltpu.make_async_remote_copy(
                    msg.at[18 + t], land.at[me_c], ssem, rsem, device_id=(me_r, dst), device_id_type=MESH
                ).start()

        @pl.when(dst == me_c)
        def _():
            for msg, land, _ssem, rsem in halves:
                pltpu.make_async_copy(msg.at[18 + t], land.at[me_c], rsem).start()


    @pl.when(is_owner)
    def _():
        resid = raw_v[pl.ds(pl.multiple_of(own_o * 8, 8), 8), :]
        c_out.wait()
        c_proj.wait()
        pltpu.make_async_copy(wrecv0, wrecv0, w0_recv).wait()
        st = wrecv0[:, :, 512:640].astype(F32).reshape(C_DEV * OWN, 128)
        m = (st + pltpu.roll(st, 96, 1)) + pltpu.roll(st, 64, 1)
        den = pltpu.roll(st, 32, 1)
        m3 = m.reshape(C_DEV, OWN, 128)
        top = jnp.max(m3, axis=0)
        fac = jnp.where(iota((C_DEV, OWN, 128), 2) < 32, jnp.exp(jnp.minimum(m3 - top[None], 0.0)), 0.0)
        whole = jnp.sum(fac * den.reshape(C_DEV, OWN, 128), axis=0)
        whole = jnp.where(iota((OWN, 128), 1) < 32, whole, 1.0)
        fac = (fac / whole[None]).reshape(C_DEV * OWN, 128)
        high = fac.astype(BF16)
        low = (fac - high.astype(F32)).astype(BF16)
        fac2_v[...] = jnp.concatenate([high, low], axis=1)
        update = resid
        for g in range(2):
            land = (wrecv0, wrecv1)[g]
            half = slice(g * 512, (g + 1) * 512)
            if g == 1:
                pltpu.make_async_copy(wrecv1, wrecv1, w1_recv).wait()
            wide = nn(fac2_v[...], expand_v[:, half]).reshape(C_DEV, OWN, 512)
            attended = jnp.sum(wide * land[:, :, 0:512].astype(F32), axis=0).astype(BF16)
            update = update + nn(attended, wout_v[half, :])
        seq_new = update.astype(BF16).astype(F32)
        proj = nn(wide_norm(seq_new).astype(BF16), wproj_v[...]).astype(BF16).astype(F32)
        turned = pltpu.roll(proj, 64, 1)
        lane8 = iota((OWN, 128), 1)
        right = jnp.where(lane8 < 64, turned, proj).astype(BF16)
        rmsg[...] = right
        slot = lax.rem(own_o, 6)
        for r in range(R_DEV):
            here = jnp.logical_and(r == me_r, dest_c == me_c)

            @pl.when(jnp.logical_not(here))
            def _():
                pltpu.make_async_remote_copy(
                    rmsg, rrecv.at[slot], r_send, r_recv, device_id=(r, dest_c), device_id_type=MESH
                ).start()

            @pl.when(here)
            def _():
                pltpu.make_async_copy(rmsg, rrecv.at[slot], r_recv).start()

        for c in range(C_DEV):
            tile = seq_new[:, (c // 4) * 128 : (c // 4) * 128 + 128]
            if c % 4 != 2:
                tile = pltpu.roll(tile, (192 - 32 * (c % 4)) % 128, 1)
            emsg[c] = jnp.where(lane8 < 64, proj, tile).astype(BF16)

        for s in range(1, C_DEV):
            dst = lax.rem(me_c + (s + 15) % 31 + 1, C_DEV)
            pltpu.make_async_remote_copy(
                emsg.at[dst], erecv.at[own_o], e_send, e_recv, device_id=(me_r, dst), device_id_type=MESH
            ).start()
        pltpu.make_async_copy(emsg.at[me_c], erecv.at[own_o], e_recv).start()

    @pl.when(jnp.logical_not(is_owner))
    def _():
        c_out.wait()
        c_proj.wait()

    pltpu.make_async_copy(mid_v, mid_h, mid_sem).wait()
    pltpu.make_async_copy(msgs.at[0 : C_DEV - 1], msgs.at[0 : C_DEV - 1], s1_send).wait()
    others = pl.ds(0, 32 * (C_DEV - 1))
    pltpu.make_async_copy(sqk0.at[others], sqk0.at[others], s0_send).wait()

    def sent_rows(i, _):
        @pl.when(col_of(block_y(lax.div(i, 6)), lax.rem(i, 6)) != me_c)
        def _():
            pltpu.make_async_copy(wmsg0.at[i], wmsg0.at[i], w0_send).wait()
            pltpu.make_async_copy(wmsg1.at[i], wmsg1.at[i], w1_send).wait()

        return 0

    lax.fori_loop(0, OWNERS, sent_rows, 0)

    pltpu.make_async_copy(rrecv, rrecv, r_recv).wait()
    right_put = pltpu.make_async_copy(rrecv, right_o, in_sem.at[0])
    right_put.start()
    pltpu.make_async_copy(erecv, erecv, e_recv).wait()
    left_put = pltpu.make_async_copy(erecv, left_o, in_sem.at[1])
    left_put.start()

    @pl.when(is_owner)
    def _():
        pltpu.make_async_copy(emsg.at[0 : C_DEV - 1], emsg.at[0 : C_DEV - 1], e_send).wait()

        def sent_right(r, _):
            @pl.when(jnp.logical_not(jnp.logical_and(r == me_r, dest_c == me_c)))
            def _():
                pltpu.make_async_copy(rmsg, rmsg, r_send).wait()

            return 0

        lax.fori_loop(0, R_DEV, sent_right, 0)
    right_put.wait()
    left_put.wait()


def pair_kernel(
    mid_h, left_h, right_h, wpair_h, out_h, seq_h,
    left_b, right_b, wpair_v, left_v, seq_v, mid_v, out_v, small_sem, in_sem, out_sem,
):
    spans = [pl.ds(k * KROWS, KROWS) for k in range(KSTEPS)]
    small = [
        pltpu.make_async_copy(src, dst, small_sem.at[k])
        for k, (src, dst) in enumerate(((left_h, left_b), (right_h, right_b), (wpair_h, wpair_v)))
    ]
    for cp in small:
        cp.start()
    fetches = [pltpu.make_async_copy(mid_h.at[r], mid_v.at[r], in_sem.at[k]) for k, r in enumerate(spans)]
    for cp in fetches:
        cp.start()
    for cp in small:
        cp.wait()
    lane = iota((NJ, C), 1)
    right = right_b[...].astype(F32).reshape(NJ, C)
    scale = jnp.where(lane < 64, right, 1.0)
    shift = jnp.where(lane < 64, 0.0, -right)
    arrived = left_b[...].astype(F32).reshape(NI, C)
    left_v[...] = jnp.where(iota((NI, C), 1) < 64, arrived, pltpu.roll(arrived, 64, 1))
    pick = jnp.where(iota((32, C), 1) == iota((32, C), 0) + 64, 1.0, 0.0).astype(BF16)
    seq_v[...] = nt(pick, left_b[...].reshape(NI, C)).astype(BF16)
    seq_put = pltpu.make_async_copy(seq_v, seq_h, small_sem.at[0])
    seq_put.start()

    def step(k, _):
        rows = pl.ds(pl.multiple_of(k * KROWS, KROWS), KROWS)
        pltpu.make_async_copy(mid_h.at[rows], mid_v.at[rows], in_sem.at[k]).wait()
        left = left_v[rows, :].reshape(KROWS, 1, C)
        feature = (left * scale[None] + shift[None]).astype(BF16).reshape(KROWS * NJ, C)
        update = nn(feature, wpair_v[...])
        mid = mid_v[rows].astype(F32).reshape(KROWS * NJ, C)
        out_v[rows] = (mid + update).astype(BF16).reshape(KROWS, NJ, C)
        pltpu.make_async_copy(out_v.at[rows], out_h.at[rows], out_sem).start()
        return 0

    lax.fori_loop(0, KSTEPS, step, 0)
    seq_put.wait()
    pltpu.make_async_copy(out_v, out_h, out_sem).wait()


def local(pair, seq, w_hidden, w_back, w_bias, w_query, w_key, w_value, w_out, w_project, w_pair):
    hbm = pl.BlockSpec(memory_space=pl.ANY)
    dma = pltpu.SemaphoreType.DMA
    mid, left, right = pl.pallas_call(
        main_kernel,
        out_shape=(
            jax.ShapeDtypeStruct((NI, NJ, C), BF16),
            jax.ShapeDtypeStruct((OWNERS, OWN, 128), BF16),
            jax.ShapeDtypeStruct((6, OWN, 128), BF16),
        ),
        in_specs=[hbm] * 10,
        out_specs=(hbm, hbm, hbm),
        scratch_shapes=[
            pltpu.VMEM((NI, NJ, C), BF16),
            pltpu.VMEM((NI, NJ, C), BF16),
            pltpu.VMEM((RC * NJ, C), BF16),
            pltpu.VMEM((RC * NJ, C), BF16),
            pltpu.VMEM((RC * NJ, C), BF16),
            pltpu.VMEM((RC * NJ, C), BF16),
            pltpu.VMEM((RC * NJ, C), BF16),
            pltpu.VMEM((RC * NJ, C), BF16),
            pltpu.VMEM((BLK * NJ, C), F32),
            pltpu.VMEM((2, 6, NI, 128), F32),
            pltpu.VMEM((8 * C, 256), BF16),
            pltpu.VMEM((32, R_DEV * NI), BF16),
            pltpu.VMEM((C, PH), BF16),
            pltpu.VMEM((PH, C), BF16),
            pltpu.VMEM((HEADS, C), BF16),
            pltpu.VMEM((D, D), BF16),
            pltpu.VMEM((D, D), BF16),
            pltpu.VMEM((D, D), BF16),
            pltpu.VMEM((D, D), BF16),
            pltpu.VMEM((D, C), BF16),
            pltpu.VMEM((32, 128), BF16),
            pltpu.VMEM((C_DEV, 32, 128), BF16),
            pltpu.VMEM((D, 128), BF16),
            pltpu.VMEM((D, 128), BF16),
            pltpu.VMEM((256, D), F32),
            pltpu.VMEM((256, D), BF16),
            pltpu.VMEM((NI, D), BF16),
            pltpu.VMEM((NJ, 2 * D), F32),
            pltpu.VMEM((2, 16 * NJ, 512), BF16),
            pltpu.VMEM((2, 16 * NJ, 512), BF16),
            pltpu.VMEM((2, NI, 16 * NJ), BF16),
            pltpu.VMEM((256, D), BF16),
            pltpu.VMEM((C_DEV * OWN, 256), BF16),
            pltpu.VMEM((OWNERS, OWN, 640), BF16),
            pltpu.VMEM((OWNERS, OWN, 512), BF16),
            pltpu.VMEM((C_DEV, OWN, 640), BF16),
            pltpu.VMEM((C_DEV, OWN, 512), BF16),
            pltpu.VMEM((C_DEV, OWN, 128), BF16),
            pltpu.VMEM((OWNERS, OWN, 128), BF16),
            pltpu.VMEM((OWN, 128), BF16),
            pltpu.VMEM((6, OWN, 128), BF16),
            dma((9,)),
            dma((STEPS,)),
            dma, dma, dma, dma, dma, dma, dma, dma, dma, dma, dma, dma, dma,
        ],
        compiler_params=pltpu.CompilerParams(
            collective_id=0, has_side_effects=True, vmem_limit_bytes=60 * 1024 * 1024
        ),
        name="trunk_main",
    )(pair, seq.T, w_hidden, w_back, w_bias.T, w_query, w_key, w_value, w_out, w_project)
    pair_out, seq_out = pl.pallas_call(
        pair_kernel,
        out_shape=(jax.ShapeDtypeStruct((NI, NJ, C), BF16), jax.ShapeDtypeStruct((32, NI), BF16)),
        in_specs=[hbm] * 4,
        out_specs=(hbm, hbm),
        scratch_shapes=[
            pltpu.VMEM((OWNERS, OWN, 128), BF16),
            pltpu.VMEM((6, OWN, 128), BF16),
            pltpu.VMEM((C, C), BF16),
            pltpu.VMEM((NI, 128), F32),
            pltpu.VMEM((32, NI), BF16),
            pltpu.VMEM((NI, NJ, C), BF16),
            pltpu.VMEM((NI, NJ, C), BF16),
            dma((3,)),
            dma((KSTEPS,)),
            dma,
        ],
        compiler_params=pltpu.CompilerParams(vmem_limit_bytes=60 * 1024 * 1024),
        name="pair_update",
    )(mid, left, right, w_pair)
    return pair_out, seq_out.T


def solution(mesh):
    return jax.shard_map(
        local,
        mesh=mesh,
        in_specs=(P("row", "col", None), P(None, "col")) + (P(),) * 9,
        out_specs=(P("row", "col", None), P("row", "col")),
        check_vma=False,
    )
```
